32 devices in a mesh: draws: 2 (over x), rows: 16 (over z, y, core).
Axes of the slice: x: 2, y: 2, z: 4, core: 2. Of those that a mesh axis runs over, the one named last changes fastest.
Arguments:
- leaf_rhs: bfloat16 [192, 256, 256], P('rows'), may hold values from -6 to 6
- separator_rhs: bfloat16 [4, 16, 256, 256], P(None, 'rows'), may hold values from -6 to 6
- leaf_inverse: bfloat16 [384, 256, 256], P(('draws', 'rows')), parts along dimension 0, as said below
- leaf_factor: bfloat16 [256, 4, 256, 256], P(('draws', 'rows')), parts along dimension 0, may hold values from -0.125 to 0.125
- separator_inverse: bfloat16 [4, 32, 256, 256], P(None, ('draws', 'rows')), parts along dimension 1, as said below
- separator_factor: bfloat16 [4, 32, 2, 256, 256], P(None, ('draws', 'rows')), parts along dimension 1, may hold values from -0.1875 to 0.1875
- block_pattern: int32 [128, 4], P('rows'), may hold values from 0 to 7, as said below
- link_row: int32 [16], P('rows'), may hold values from 8 to 11
Outputs:
- leaf_solution: bfloat16 [384, 256, 256], P(('draws', 'rows')), parts along dimension 0
- separator_solution: bfloat16 [4, 32, 256, 256], P(None, ('draws', 'rows')), parts along dimension 1
The draws below stay inside these ranges and needn't reach their ends.
There are 2 independent parts, one for each index of `draws`. The reference program is written for one: setup_inputs(seed, part) draws one part's arguments, and reference() takes and returns one part's arrays. A program takes and returns all parts, laid end to end along the dimension named above; an argument that names none is the same for every part. Nothing has to cross between parts.
Inputs may be any that keep to these rules, and one draw needn't show every extreme that they name: `block_pattern`: for a block row on leaf level v >= 1 the 4 entries are distinct and below v * 4. `leaf_inverse`: every block is invertible. `separator_inverse`: every block is invertible.
All inputs are finite; a program needn't handle non-finite values.
Results may differ from the reference program's by a relative error of at most 0.011.
Values may be sent and summed in bfloat16 or wider, within the bound.
No kernel may reach another device: no remote copies, remote signals or barrier semaphores. Data moves between devices by JAX's collectives and lax.ppermute only.
A program may use at most 64 MiB of HBM per device.

```python
import math
import jax
import jax.numpy as jnp
from jax import lax

BLOCK = 256
LOADS = 256
LEVEL_ROWS = 4
LEAF_LEVELS = 3
COUPLED = 4
LOCAL = 12
UPPER = 8
LEAF_ROWS = 192
TREE_DEPTH = 4
N_ROWS = 16


def draw_dominant(key, count):
    key_diag, key_off = jax.random.split(key)
    diagonal_part = jnp.exp(jax.random.uniform(key_diag, (count, BLOCK), jnp.float32, math.log(0.5), math.log(1.5)))
    off_part = jax.random.normal(key_off, (count, BLOCK, BLOCK), jnp.float32) * (0.4 / math.sqrt(BLOCK))
    identity = jnp.eye(BLOCK, dtype=jnp.float32)
    return (off_part + identity[None, :, :] * diagonal_part[:, :, None]).astype(jnp.bfloat16)


def draw_leaf_inverse(key, part):
    return draw_dominant(jax.random.fold_in(key, 11), N_ROWS * LOCAL)


def draw_separator_inverse(key, part):
    return draw_dominant(jax.random.fold_in(key, 23), TREE_DEPTH * N_ROWS).reshape(TREE_DEPTH, N_ROWS, BLOCK, BLOCK)


def draw_block_pattern(key, part):
    total_rows = N_ROWS * UPPER
    scores = jax.random.randint(jax.random.fold_in(key, 37), (total_rows, UPPER), 0, 2 ** 20, dtype=jnp.int32)
    column = jnp.arange(UPPER, dtype=jnp.int32)[None, :]
    leaf_level = jnp.arange(total_rows, dtype=jnp.int32) % UPPER // LEVEL_ROWS + 1
    available = (leaf_level * LEVEL_ROWS)[:, None]
    keyed = scores * UPPER + column + jnp.where(column >= available, 2 ** 30, 0).astype(jnp.int32)
    ordered = jnp.argsort(keyed, axis=1, stable=True)
    return ordered[:, :COUPLED].astype(jnp.int32)


def place_ends(values, own_key, low, top_value):
    spot = [jax.random.randint(jax.random.fold_in(own_key, axis), (), 0, length) for axis, length in enumerate(values.shape)]
    longest = values.shape.index(max(values.shape))
    neighbour = spot[:longest] + [(spot[longest] + 1) % values.shape[longest]] + spot[longest + 1:]
    return values.at[tuple(spot)].set(low).at[tuple(neighbour)].set(top_value)


def block_scale(own_key, extent, shards, smallest, largest):
    def one(position, shards_of):
        steps = jax.random.uniform(jax.random.fold_in(jax.random.fold_in(own_key, 6), position), (shards_of,), jnp.float32, smallest / len(shards), largest / len(shards))
        return jnp.repeat(jnp.exp(steps), extent[position] // shards_of).reshape((-1,) + (1,) * (len(extent) - position - 1))

    level = one(*shards[0])
    for cut in shards[1:]:
        level = level * one(*cut)
    return level


def scatter_about(own_key, shape, spread, bound, cuts=(), held_as=jnp.bfloat16):
    level = block_scale(own_key, shape, cuts, -0.22, 0.18) if cuts else 1.0
    result = jax.random.normal(own_key, shape, jnp.float32) * spread * level
    return jnp.minimum(jnp.maximum(result, -bound), bound).astype(held_as)


def setup_inputs(seed: int = 0, part: int = 0) -> dict:
    key_of = jax.random.split(jax.random.key(seed), 9)
    own_keys = jax.random.split(jax.random.fold_in(key_of[8], part), 9)
    return {
        "leaf_rhs": scatter_about(key_of[0], (LEAF_ROWS, BLOCK, LOADS), 1.0, 6.0, ((0, 16),)),
        "separator_rhs": scatter_about(key_of[1], (TREE_DEPTH, N_ROWS, BLOCK, LOADS), 1.0, 6.0, ((1, 16),)),
        "leaf_inverse": draw_leaf_inverse(jax.random.fold_in(jax.random.fold_in(key_of[8], part), 71), part),
        "leaf_factor": scatter_about(own_keys[3], (UPPER * N_ROWS, COUPLED, BLOCK, BLOCK), (2 * COUPLED * BLOCK) ** -0.5, 0.125, ((0, 16),)),
        "separator_inverse": draw_separator_inverse(jax.random.fold_in(jax.random.fold_in(key_of[8], part), 71), part),
        "separator_factor": scatter_about(own_keys[5], (TREE_DEPTH, N_ROWS, 2, BLOCK, BLOCK), (4 * BLOCK) ** -0.5, 0.1875, ((1, 16),)),
        "block_pattern": draw_block_pattern(jax.random.fold_in(key_of[8], 71), part),
        "link_row": place_ends(jax.random.randint(key_of[7], (N_ROWS,), UPPER, LOCAL), jax.random.fold_in(key_of[7], 1), UPPER, LOCAL - 1).astype(jnp.int32),
    }


def solve_leaf(leaf_items):
    rhs_one, inverse_one, factor_one, pattern_one = leaf_items
    solved = jnp.einsum("nij,njr->nir", inverse_one[:LEVEL_ROWS].astype(jnp.float32), rhs_one[:LEVEL_ROWS].astype(jnp.float32)).astype(jnp.bfloat16)
    for height in range(1, LEAF_LEVELS):
        low_row = (height - 1) * LEVEL_ROWS
        top_row = height * LEVEL_ROWS
        picked = jnp.take(solved, pattern_one[low_row:top_row], axis=0)
        accumulated = jnp.einsum("nkij,nkjr->nir", factor_one[low_row:top_row].astype(jnp.float32), picked.astype(jnp.float32))
        residual = (rhs_one[top_row:top_row + LEVEL_ROWS].astype(jnp.float32) - accumulated).astype(jnp.bfloat16)
        fresh_rows = jnp.einsum("nij,njr->nir", inverse_one[top_row:top_row + LEVEL_ROWS].astype(jnp.float32), residual.astype(jnp.float32)).astype(jnp.bfloat16)
        solved = jnp.concatenate([solved, fresh_rows], axis=0)
    return solved


def solve_level(lower_in, upper_in, rhs_level, inverse_level, factor_level):
    factors = factor_level.astype(jnp.float32)
    accumulated = jnp.einsum("nij,njr->nir", factors[:, 0], lower_in.astype(jnp.float32)) + jnp.einsum("nij,njr->nir", factors[:, 1], upper_in.astype(jnp.float32))
    residual = (rhs_level.astype(jnp.float32) - accumulated).astype(jnp.bfloat16)
    return jnp.einsum("nij,njr->nir", inverse_level.astype(jnp.float32), residual.astype(jnp.float32)).astype(jnp.bfloat16)


def reference(leaf_rhs, separator_rhs, leaf_inverse, leaf_factor, separator_inverse, separator_factor, block_pattern, link_row):
    leaf_items = (leaf_rhs.reshape(N_ROWS, LOCAL, BLOCK, LOADS), leaf_inverse.reshape(N_ROWS, LOCAL, BLOCK, BLOCK), leaf_factor.reshape(N_ROWS, UPPER, COUPLED, BLOCK, BLOCK), block_pattern.reshape(N_ROWS, UPPER, COUPLED))
    solved = lax.map(solve_leaf, leaf_items)
    edges = solved[jnp.arange(N_ROWS, dtype=jnp.int32), link_row]
    level_block = solve_level(jnp.roll(edges, 1, axis=0), edges, separator_rhs[0], separator_inverse[0], separator_factor[0])
    levels = [level_block]
    for height in range(1, TREE_DEPTH):
        stride = 2 ** (height - 1)
        level_block = solve_level(jnp.roll(level_block, stride, axis=0), jnp.roll(level_block, -stride, axis=0), separator_rhs[height], separator_inverse[height], separator_factor[height])
        levels.append(level_block)
    return solved.reshape(N_ROWS * LOCAL, BLOCK, LOADS), jnp.stack(levels, axis=0)
```

```python
import functools

import jax
import jax.numpy as jnp
from jax import lax
from jax.experimental import pallas as pl
from jax.experimental.pallas import tpu as pltpu
from jax.sharding import PartitionSpec as P

LEVEL_ROWS = 4
LEAF_LEVELS = 3
F32 = jnp.float32
BF16 = jnp.bfloat16

VMEM = pl.BlockSpec(memory_space=pltpu.VMEM)
HBM = pl.BlockSpec(memory_space=pltpu.HBM)
SMEM = pl.BlockSpec(memory_space=pltpu.SMEM)


def passed_along(value, axis, by):
    length = lax.axis_size(axis)
    return lax.ppermute(value, axis, [(i, (i + by) % length) for i in range(length)])


def mm(a, b):
    return jnp.dot(a, b, preferred_element_type=F32)


def leaf_row(factor, solved, pattern, row, coupled, rhs, inverse):
    total = rhs.astype(F32)
    for k in range(coupled):
        total = total - mm(factor[k], solved[pattern[row, k]])
    return mm(inverse, total.astype(BF16)).astype(BF16)


def edge_kernel(pattern, link, rhs, inverse, factor, solved, edge, rhs_v, inv_v, fac_v, top_fac, sem):
    coupled = factor.shape[1]
    n = LEVEL_ROWS
    low = 2 * n
    top = link[0]

    def load(src, dst, slot):
        copy = pltpu.make_async_copy(src, dst, sem.at[slot])
        copy.start()
        return copy

    first_inv = load(inverse.at[pl.ds(0, n)], inv_v.at[pl.ds(0, n)], 0)
    first_rhs = load(rhs.at[pl.ds(0, n)], rhs_v.at[pl.ds(0, n)], 1)
    rows = []
    for r in range(n):
        rows.append(
            (
                load(factor.at[r], fac_v.at[r], 2 + 3 * r),
                load(rhs.at[n + r], rhs_v.at[n + r], 3 + 3 * r),
                load(inverse.at[n + r], inv_v.at[n + r], 4 + 3 * r),
            )
        )
    base = 2 + 3 * n
    last = (
        load(factor.at[top - n], top_fac, base),
        load(rhs.at[top], rhs_v.at[low], base + 1),
        load(inverse.at[top], inv_v.at[low], base + 2),
    )
    first_inv.wait()
    first_rhs.wait()
    for r in range(n):
        solved[r] = mm(inv_v[r], rhs_v[r]).astype(BF16)
    for r in range(n):
        for copy in rows[r]:
            copy.wait()
        solved[n + r] = leaf_row(
            fac_v[r], solved, pattern, r, coupled, rhs_v[n + r], inv_v[n + r]
        )
    for copy in last:
        copy.wait()
    edge[...] = leaf_row(top_fac, solved, pattern, top - n, coupled, rhs_v[low], inv_v[low])


def edge_call(pattern, link, rhs, inverse, factor):
    n = LEVEL_ROWS
    coupled, block = factor.shape[1], factor.shape[2]
    loads = rhs.shape[-1]
    return pl.pallas_call(
        edge_kernel,
        out_shape=(
            jax.ShapeDtypeStruct((2 * n, block, loads), BF16),
            jax.ShapeDtypeStruct((block, loads), BF16),
        ),
        in_specs=[SMEM, SMEM, HBM, HBM, HBM],
        out_specs=(VMEM, VMEM),
        scratch_shapes=[
            pltpu.VMEM((2 * n + 1, block, loads), BF16),
            pltpu.VMEM((2 * n + 1, block, block), BF16),
            pltpu.VMEM((n, coupled, block, block), BF16),
            pltpu.VMEM((coupled, block, block), BF16),
            pltpu.SemaphoreType.DMA((5 + 3 * n,)),
        ],
        compiler_params=pltpu.CompilerParams(vmem_limit_bytes=16 << 20),
        name="leaf_edge",
    )(pattern, link, rhs, inverse, factor)


def rest_kernel(pattern, rhs, inverse, factor, low, solved, rhs_v, inv_v, fac_v, top, sem):
    coupled = factor.shape[1]
    n = LEVEL_ROWS

    def start(src, dst, slot):
        copy = pltpu.make_async_copy(src, dst, sem.at[slot])
        copy.start()
        return copy

    rhs_in = start(rhs.at[pl.ds(2 * n, n)], rhs_v, 0)
    inv_in = start(inverse.at[pl.ds(2 * n, n)], inv_v, 1)
    fac_in = [start(factor.at[n + r], fac_v.at[r], 3 + r) for r in range(n)]
    low_out = start(low, solved.at[pl.ds(0, 2 * n)], 2)
    rhs_in.wait()
    inv_in.wait()
    for r in range(n):
        fac_in[r].wait()
        top[r] = leaf_row(fac_v[r], low, pattern, n + r, coupled, rhs_v[r], inv_v[r])
    start(top, solved.at[pl.ds(2 * n, n)], 0).wait()
    low_out.wait()


def rest_call(pattern, rhs, inverse, factor, low):
    n = LEVEL_ROWS
    coupled, block = factor.shape[1], factor.shape[2]
    loads = rhs.shape[-1]
    flops = 2 * n * (coupled + 1) * block * block * loads
    return pl.pallas_call(
        rest_kernel,
        out_shape=jax.ShapeDtypeStruct((LEAF_LEVELS * n, block, loads), BF16),
        in_specs=[SMEM, HBM, HBM, HBM, VMEM],
        out_specs=HBM,
        scratch_shapes=[
            pltpu.VMEM((n, block, loads), BF16),
            pltpu.VMEM((n, block, block), BF16),
            pltpu.VMEM((n, coupled, block, block), BF16),
            pltpu.VMEM((n, block, loads), BF16),
            pltpu.SemaphoreType.DMA((3 + n,)),
        ],
        cost_estimate=pl.CostEstimate(
            flops=flops, bytes_accessed=36 * block * block * 2, transcendentals=0
        ),
        compiler_params=pltpu.CompilerParams(vmem_limit_bytes=16 << 20),
        name="leaf_rest",
    )(pattern, rhs, inverse, factor, low)


def fold_kernel(rhs, inverse, factor, lower_mat, upper_mat, const):
    for h in range(rhs.shape[0]):
        inv = inverse[h, 0]
        lower_mat[h] = mm(inv, factor[h, 0, 0]).astype(BF16)
        upper_mat[h] = mm(inv, factor[h, 0, 1]).astype(BF16)
        const[h] = mm(inv, rhs[h, 0])


def fold_call(rhs, inverse, factor):
    depth, _, block, loads = rhs.shape
    return pl.pallas_call(
        fold_kernel,
        out_shape=(
            jax.ShapeDtypeStruct((depth, block, block), BF16),
            jax.ShapeDtypeStruct((depth, block, block), BF16),
            jax.ShapeDtypeStruct((depth, block, loads), F32),
        ),
        in_specs=[VMEM, VMEM, VMEM],
        out_specs=(VMEM, VMEM, VMEM),
        cost_estimate=pl.CostEstimate(
            flops=6 * depth * block * block * loads,
            bytes_accessed=8 * depth * block * block * 2,
            transcendentals=0,
        ),
        compiler_params=pltpu.CompilerParams(vmem_limit_bytes=16 << 20),
        name="fold",
    )(rhs, inverse, factor)


def node_kernel(h, lower, upper, lower_mat, upper_mat, const, out):
    total = const[h] - mm(upper_mat[h], upper[...]) - mm(lower_mat[h], lower[...])
    out[...] = total.astype(BF16)


def node_call(h, lower, upper, lower_mat, upper_mat, const):
    return pl.pallas_call(
        functools.partial(node_kernel, h),
        out_shape=jax.ShapeDtypeStruct(lower.shape, BF16),
        in_specs=[VMEM] * 5,
        out_specs=VMEM,
        compiler_params=pltpu.CompilerParams(vmem_limit_bytes=8 << 20),
        name=f"node{h}",
    )(lower, upper, lower_mat, upper_mat, const)


def shards(
    leaf_rhs,
    separator_rhs,
    leaf_inverse,
    leaf_factor,
    separator_inverse,
    separator_factor,
    block_pattern,
    link_row,
):
    low, edge = edge_call(block_pattern, link_row, leaf_rhs, leaf_inverse, leaf_factor)
    lower = passed_along(edge, "rows", 1)
    solved = rest_call(block_pattern, leaf_rhs, leaf_inverse, leaf_factor, low)
    mats = fold_call(separator_rhs, separator_inverse, separator_factor)
    block = node_call(0, lower, edge, *mats)
    levels = [block]
    for height in range(1, separator_rhs.shape[0]):
        stride = 2 ** (height - 1)
        lower = passed_along(block, "rows", stride)
        upper = passed_along(block, "rows", -stride)
        block = node_call(height, lower, upper, *mats)
        levels.append(block)
    return solved, jnp.stack(levels, axis=0)[:, None]


def solution(mesh):
    placed = (
        P("rows", None, None),
        P(None, "rows", None, None),
        P(("draws", "rows"), None, None),
        P(("draws", "rows"), None, None, None),
        P(None, ("draws", "rows"), None, None),
        P(None, ("draws", "rows"), None, None, None),
        P("rows", None),
        P("rows"),
    )
    return jax.shard_map(
        shards,
        mesh=mesh,
        in_specs=placed,
        out_specs=(P(("draws", "rows"), None, None), P(None, ("draws", "rows"), None, None)),
        check_vma=False,
    )
```

```python
import functools

import jax
import jax.numpy as jnp
from jax import lax
from jax.experimental import pallas as pl
from jax.experimental.pallas import tpu as pltpu
from jax.sharding import PartitionSpec as P

LEVEL_ROWS = 4
LEAF_LEVELS = 3
F32 = jnp.float32
BF16 = jnp.bfloat16

SMEM = pl.BlockSpec(memory_space=pltpu.SMEM)
VMEM = pl.BlockSpec(memory_space=pltpu.VMEM)
HBM = pl.BlockSpec(memory_space=pltpu.HBM)


def passed_along(value, axis, by):
    length = lax.axis_size(axis)
    return lax.ppermute(value, axis, [(i, (i + by) % length) for i in range(length)])


def in_hbm(array):
    return pltpu.with_memory_space_constraint(array, pltpu.HBM)


def mm(a, b):
    return jnp.dot(a, b, preferred_element_type=F32)


def leaf_residual(factor, solved, pattern, row, rhs):
    coupled = factor.shape[0]
    wide = jnp.concatenate([factor[k] for k in range(coupled)], axis=1)
    tall = jnp.concatenate([solved[pattern[k, row]] for k in range(coupled)], axis=0)
    return (rhs.astype(F32) - mm(wide, tall)).astype(BF16)


def pair_swap(value, axis):
    length = lax.axis_size(axis)
    return lax.ppermute(value, axis, [(i, i ^ 1) for i in range(length)])


def border_swap(value, axis):
    length = lax.axis_size(axis)
    pairs = [(i, (i + (1 if i % 2 else -1)) % length) for i in range(length)]
    return lax.ppermute(value, axis, pairs)


def on_odd():
    return lax.rem(lax.axis_index("rows"), 2) == 1


def edge_kernel(
    columns, link, rhs, inverse, factor, node_rhs, node_inverse, node_factor,
    solved, edge, sent, lower_mat, upper_mat, const,
    pattern, rhs_v, inv_v, fac_v, top_fac, left, node_r, node_i, node_f, sem,
):
    n = LEVEL_ROWS
    low = 2 * n
    slots = iter(range(sem.shape[0]))

    def load(src, dst):
        copy = pltpu.make_async_copy(src, dst, sem.at[next(slots)])
        copy.start()
        return copy

    first_inv = load(inverse.at[pl.ds(0, n)], inv_v.at[pl.ds(0, n)])
    first_rhs = load(rhs.at[pl.ds(0, n)], rhs_v.at[pl.ds(0, n)])
    pattern_in = load(columns, pattern)
    next_rhs = load(rhs.at[pl.ds(n, n)], rhs_v.at[pl.ds(n, n)])
    next_fac = [load(factor.at[r], fac_v.at[r]) for r in range(n)]
    next_inv = load(inverse.at[pl.ds(n, n)], inv_v.at[pl.ds(n, n)])
    node_in = (
        load(node_inverse.at[0, 0], node_i),
        load(node_factor.at[0, 0], node_f),
        load(node_rhs.at[0, 0], node_r),
    )
    top = link[0]
    last = (
        load(factor.at[top - n], top_fac),
        load(rhs.at[top], rhs_v.at[low]),
        load(inverse.at[top], inv_v.at[low]),
    )
    first_inv.wait()
    first_rhs.wait()
    for r in range(n):
        solved[r] = mm(inv_v[r], rhs_v[r]).astype(BF16)
    pattern_in.wait()
    next_rhs.wait()
    for r in range(n):
        next_fac[r].wait()
        left[r] = leaf_residual(fac_v.at[r], solved, pattern, r, rhs_v[n + r])
    next_inv.wait()
    for r in range(n):
        solved[n + r] = mm(inv_v[n + r], left[r]).astype(BF16)
    for copy in node_in:
        copy.wait()
    lower_mat[...] = mm(node_i[...], node_f[0]).astype(BF16)
    upper_mat[...] = mm(node_i[...], node_f[1]).astype(BF16)
    const[...] = mm(node_i[...], node_r[...])
    for copy in last:
        copy.wait()
    residual = leaf_residual(top_fac, solved, pattern, top - n, rhs_v[low])
    edge_value = mm(inv_v[low], residual).astype(BF16)
    edge[...] = edge_value
    odd = on_odd()

    @pl.when(odd)
    def _():
        sent[...] = edge_value

    @pl.when(jnp.logical_not(odd))
    def _():
        sent[...] = (const[...] - mm(upper_mat[...], edge_value)).astype(BF16)


def edge_call(pattern, link, rhs, inverse, factor, node_rhs, node_inverse, node_factor):
    n = LEVEL_ROWS
    coupled, block = factor.shape[1], factor.shape[2]
    loads = rhs.shape[-1]
    return pl.pallas_call(
        edge_kernel,
        out_shape=(
            pltpu.VMEM((2 * n, block, loads), BF16),
            pltpu.VMEM((block, loads), BF16),
            pltpu.VMEM((block, loads), BF16),
            pltpu.VMEM((block, block), BF16),
            pltpu.VMEM((block, block), BF16),
            pltpu.VMEM((block, loads), F32),
        ),
        in_specs=[HBM, SMEM] + [HBM] * 6,
        out_specs=(VMEM,) * 6,
        scratch_shapes=[
            pltpu.SMEM(pattern.shape, jnp.int32),
            pltpu.VMEM((2 * n + 1, block, loads), BF16),
            pltpu.VMEM((2 * n + 1, block, block), BF16),
            pltpu.VMEM((n, coupled, block, block), BF16),
            pltpu.VMEM((coupled, block, block), BF16),
            pltpu.VMEM((n, block, loads), BF16),
            pltpu.VMEM((block, loads), BF16),
            pltpu.VMEM((block, block), BF16),
            pltpu.VMEM((2, block, block), BF16),
            pltpu.SemaphoreType.DMA((11 + n,)),
        ],
        compiler_params=pltpu.CompilerParams(vmem_limit_bytes=16 << 20),
        name="leaf_edge",
    )(
        in_hbm(pattern), link, in_hbm(rhs), in_hbm(inverse), in_hbm(factor),
        in_hbm(node_rhs), in_hbm(node_inverse), in_hbm(node_factor),
    )


def early_kernel(lower, upper, lower_mat, upper_mat, const, out):
    odd = on_odd()

    @pl.when(odd)
    def _():
        total = const[...] - mm(upper_mat[...], upper[...]) - mm(lower_mat[...], lower[...])
        out[...] = total.astype(BF16)

    @pl.when(jnp.logical_not(odd))
    def _():
        out[...] = lower_mat[...]


def late_kernel(part, lower, early, lower_mat, *rest):
    out = rest[-1]
    odd = on_odd()

    @pl.when(odd)
    def _():
        out[...] = early[...]

    @pl.when(jnp.logical_not(odd))
    def _():
        out[...] = (part[...].astype(F32) - mm(lower_mat[...], lower[...])).astype(BF16)


def level_one_kernel(inner, came_first, came_next, edge, lower_mat, upper_mat, const, out):
    odd = on_odd()

    @pl.when(odd)
    def _():
        upper = came_first[...].astype(F32) - mm(came_next[...], edge[...])
        total = const[0] - mm(lower_mat[0], inner[...]) - mm(upper_mat[0], upper.astype(BF16))
        out[...] = total.astype(BF16)

    @pl.when(jnp.logical_not(odd))
    def _():
        total = const[0] - mm(upper_mat[0], inner[...]) - mm(lower_mat[0], came_next[...])
        out[...] = total.astype(BF16)


def small_call(kernel, name, shape, *args):
    return pl.pallas_call(
        kernel,
        out_shape=pltpu.VMEM(shape, BF16),
        in_specs=[VMEM] * len(args),
        out_specs=VMEM,
        compiler_params=pltpu.CompilerParams(vmem_limit_bytes=8 << 20),
        name=name,
    )(*args)


def rest_kernel(columns, rhs, inverse, factor, low, top, pattern, rhs_v, inv_v, fac_v, left, sem):
    n = LEVEL_ROWS

    def load(src, dst, slot):
        copy = pltpu.make_async_copy(src, dst, sem.at[slot])
        copy.start()
        return copy

    pattern_in = load(columns, pattern, 0)
    rhs_in = load(rhs.at[pl.ds(2 * n, n)], rhs_v, 1)
    fac_in = [load(factor.at[n + r], fac_v.at[r], 3 + r) for r in range(n)]
    inv_in = load(inverse.at[pl.ds(2 * n, n)], inv_v, 2)
    pattern_in.wait()
    rhs_in.wait()
    for r in range(n):
        fac_in[r].wait()
        left[r] = leaf_residual(fac_v.at[r], low, pattern, n + r, rhs_v[r])
    inv_in.wait()
    for r in range(n):
        top[r] = mm(inv_v[r], left[r]).astype(BF16)


def rest_call(pattern, rhs, inverse, factor, low):
    n = LEVEL_ROWS
    coupled, block = factor.shape[1], factor.shape[2]
    loads = rhs.shape[-1]
    flops = 2 * n * (coupled + 1) * block * block * loads
    return pl.pallas_call(
        rest_kernel,
        out_shape=pltpu.VMEM((n, block, loads), BF16),
        in_specs=[HBM] * 4 + [VMEM],
        out_specs=VMEM,
        scratch_shapes=[
            pltpu.SMEM(pattern.shape, jnp.int32),
            pltpu.VMEM((n, block, loads), BF16),
            pltpu.VMEM((n, block, block), BF16),
            pltpu.VMEM((n, coupled, block, block), BF16),
            pltpu.VMEM((n, block, loads), BF16),
            pltpu.SemaphoreType.DMA((3 + n,)),
        ],
        compiler_params=pltpu.CompilerParams(vmem_limit_bytes=12 << 20),
        cost_estimate=pl.CostEstimate(
            flops=flops, bytes_accessed=36 * block * block * 2, transcendentals=0
        ),
        name="leaf_rest",
    )(in_hbm(pattern), in_hbm(rhs), in_hbm(inverse), in_hbm(factor), low)


def fold_kernel(rhs, inverse, factor, _, lower_mat, upper_mat, const):
    for h in range(1, rhs.shape[0]):
        inv = inverse[h, 0]
        lower_mat[h - 1] = mm(inv, factor[h, 0, 0]).astype(BF16)
        upper_mat[h - 1] = mm(inv, factor[h, 0, 1]).astype(BF16)
        const[h - 1] = mm(inv, rhs[h, 0])


def fold_call(rhs, inverse, factor, after):
    depth, _, block, loads = rhs.shape
    depth = depth - 1
    return pl.pallas_call(
        fold_kernel,
        out_shape=(
            pltpu.VMEM((depth, block, block), BF16),
            pltpu.VMEM((depth, block, block), BF16),
            pltpu.VMEM((depth, block, loads), F32),
        ),
        in_specs=[VMEM] * 4,
        out_specs=(VMEM, VMEM, VMEM),
        cost_estimate=pl.CostEstimate(
            flops=6 * depth * block * block * loads,
            bytes_accessed=8 * depth * block * block * 2,
            transcendentals=0,
        ),
        compiler_params=pltpu.CompilerParams(vmem_limit_bytes=16 << 20),
        name="fold",
    )(rhs, inverse, factor, after)


def node_kernel(h, lower, upper, lower_mat, upper_mat, const, out):
    total = const[h] - mm(upper_mat[h], upper[...]) - mm(lower_mat[h], lower[...])
    out[...] = total.astype(BF16)


def collect_kernel(low, top, *refs):
    *levels, solved, out, sem = refs
    copies = [
        pltpu.make_async_copy(level, out.at[h, 0], sem.at[h]) for h, level in enumerate(levels)
    ]
    n = low.shape[0]
    h = len(levels)
    copies.append(pltpu.make_async_copy(low, solved.at[pl.ds(0, n)], sem.at[h]))
    copies.append(pltpu.make_async_copy(top, solved.at[pl.ds(n, top.shape[0])], sem.at[h + 1]))
    for copy in copies:
        copy.start()
    for copy in copies:
        copy.wait()


def collect_call(low, top, levels, shape):
    rows = low.shape[0] + top.shape[0]
    return pl.pallas_call(
        collect_kernel,
        out_shape=(
            jax.ShapeDtypeStruct((rows,) + low.shape[1:], BF16),
            jax.ShapeDtypeStruct(shape, BF16),
        ),
        in_specs=[VMEM] * (2 + len(levels)),
        out_specs=(HBM, HBM),
        scratch_shapes=[pltpu.SemaphoreType.DMA((2 + len(levels),))],
        compiler_params=pltpu.CompilerParams(vmem_limit_bytes=4 << 20),
        cost_estimate=pl.CostEstimate(
            flops=0,
            bytes_accessed=(rows + len(levels)) * shape[2] * shape[3] * 4,
            transcendentals=0,
        ),
        name="collect",
    )(low, top, *levels)


def last_kernel(lower, upper, lower_mat, upper_mat, const, _, out, piece, sem):
    h = const.shape[0] - 1
    rows = const.shape[1] // 2
    copies = []
    for half in range(2):
        part = pl.ds(half * rows, rows)
        total = (
            const[h, part]
            - mm(upper_mat[h, part], upper[...])
            - mm(lower_mat[h, part], lower[...])
        )
        piece[part] = total.astype(BF16)
        copy = pltpu.make_async_copy(
            piece.at[part], out.at[out.shape[0] - 1, 0, part], sem.at[half]
        )
        copy.start()
        copies.append(copy)
    for copy in copies:
        copy.wait()


def last_call(lower, upper, lower_mat, upper_mat, const, collected):
    return pl.pallas_call(
        last_kernel,
        out_shape=jax.ShapeDtypeStruct(collected.shape, BF16),
        in_specs=[VMEM] * 5 + [HBM],
        out_specs=HBM,
        input_output_aliases={5: 0},
        scratch_shapes=[pltpu.VMEM(lower.shape, BF16), pltpu.SemaphoreType.DMA((2,))],
        compiler_params=pltpu.CompilerParams(vmem_limit_bytes=8 << 20),
        name="node_last",
    )(lower, upper, lower_mat, upper_mat, const, collected)


def shards(
    leaf_rhs,
    separator_rhs,
    leaf_inverse,
    leaf_factor,
    separator_inverse,
    separator_factor,
    block_pattern,
    link_row,
):
    columns = block_pattern.T
    low, edge, sent, lower_mat, upper_mat, const = edge_call(
        columns, link_row, leaf_rhs, leaf_inverse, leaf_factor,
        separator_rhs, separator_inverse, separator_factor,
    )
    shape = edge.shape
    edge_inner = pair_swap(edge, "rows")
    came_first = border_swap(sent, "rows")
    early = small_call(
        early_kernel, "level0_early", shape, edge_inner, edge, lower_mat, upper_mat, const
    )
    came_next = border_swap(early, "rows")
    top = rest_call(columns, leaf_rhs, leaf_inverse, leaf_factor, low)
    mats = fold_call(separator_rhs, separator_inverse, separator_factor, early)
    block = small_call(
        late_kernel, "level0_late", shape, sent, came_first, early, lower_mat, came_next, top, mats[2],
    )
    inner = pair_swap(block, "rows")
    levels = [block]
    block = small_call(
        level_one_kernel, "level1", shape, inner, came_first, came_next, edge, *mats
    )
    levels.append(block)
    depth = separator_rhs.shape[0]
    for height in range(2, depth):
        stride = 2 ** (height - 1)
        lower = passed_along(block, "rows", stride)
        upper = passed_along(block, "rows", -stride)
        if height < depth - 1:
            step = functools.partial(node_kernel, height - 1)
            block = small_call(step, f"level{height}", shape, lower, upper, *mats)
            levels.append(block)
    solved, collected = collect_call(low, top, levels, (depth, 1) + shape)
    return solved, last_call(lower, upper, *mats, collected)


def solution(mesh):
    placed = (
        P("rows", None, None),
        P(None, "rows", None, None),
        P(("draws", "rows"), None, None),
        P(("draws", "rows"), None, None, None),
        P(None, ("draws", "rows"), None, None),
        P(None, ("draws", "rows"), None, None, None),
        P("rows", None),
        P("rows"),
    )
    return jax.shard_map(
        shards,
        mesh=mesh,
        in_specs=placed,
        out_specs=(P(("draws", "rows"), None, None), P(None, ("draws", "rows"), None, None)),
        check_vma=False,
    )
```

```python
import functools

import jax
import jax.numpy as jnp
from jax import lax
from jax.experimental import pallas as pl
from jax.experimental.pallas import tpu as pltpu
from jax.sharding import PartitionSpec as P

LEVEL_ROWS = 4
LEAF_LEVELS = 3
F32 = jnp.float32
BF16 = jnp.bfloat16

SMEM = pl.BlockSpec(memory_space=pltpu.SMEM)
VMEM = pl.BlockSpec(memory_space=pltpu.VMEM)
HBM = pl.BlockSpec(memory_space=pltpu.HBM)


def passed_along(value, axis, by):
    length = lax.axis_size(axis)
    return lax.ppermute(value, axis, [(i, (i + by) % length) for i in range(length)])


def in_hbm(array):
    return pltpu.with_memory_space_constraint(array, pltpu.HBM)


def mm(a, b):
    return jnp.dot(a, b, preferred_element_type=F32)


def leaf_residual(factor, solved, pattern, row, rhs):
    coupled = factor.shape[0]
    wide = jnp.concatenate([factor[k] for k in range(coupled)], axis=1)
    tall = jnp.concatenate([solved[pattern[k, row]] for k in range(coupled)], axis=0)
    return (rhs.astype(F32) - mm(wide, tall)).astype(BF16)


def pair_swap(value, axis):
    length = lax.axis_size(axis)
    return lax.ppermute(value, axis, [(i, i ^ 1) for i in range(length)])


def edge_kernel(
    columns, link, rhs, inverse, factor, node_rhs, node_inverse, node_factor,
    solved, edge, down,
    pattern, rhs_v, inv_v, fac_v, top_fac, left, both, const, node_r, node_i, node_f, sem,
):
    n = LEVEL_ROWS
    low = 2 * n
    block = factor.shape[2]
    slots = iter(range(sem.shape[0]))

    def load(src, dst):
        copy = pltpu.make_async_copy(src, dst, sem.at[next(slots)])
        copy.start()
        return copy

    top = link[0]
    first_in = (
        load(inverse.at[pl.ds(0, n)], inv_v.at[pl.ds(0, n)]),
        load(rhs.at[pl.ds(0, n)], rhs_v.at[pl.ds(0, n)]),
    )
    node_in = (
        load(node_inverse.at[0, 0], node_i),
        load(node_factor.at[0, 0], node_f),
        load(node_rhs.at[0, 0], node_r),
        load(inverse.at[top], both.at[pl.ds(0, block)]),
    )
    next_in = (
        load(columns, pattern),
        load(rhs.at[pl.ds(n, n)], rhs_v.at[pl.ds(n, n)]),
        load(inverse.at[pl.ds(n, n)], inv_v.at[pl.ds(n, n)]),
        load(factor.at[pl.ds(0, n)], fac_v),
    )
    last_in = (
        load(rhs.at[top], rhs_v.at[low]),
        load(factor.at[top - n], top_fac),
    )
    for copy in first_in:
        copy.wait()
    for r in range(n):
        solved[r] = mm(inv_v[r], rhs_v[r]).astype(BF16)
    for copy in node_in:
        copy.wait()
    down[1] = mm(node_i[...], node_f[0]).astype(BF16)
    upper = mm(node_i[...], node_f[1]).astype(BF16)
    const[...] = mm(node_i[...], node_r[...])
    both[pl.ds(block, block)] = mm(upper, both[pl.ds(0, block)]).astype(BF16)
    for copy in next_in:
        copy.wait()
    for r in range(n):
        left[r] = leaf_residual(fac_v.at[r], solved, pattern, r, rhs_v[n + r])
    for r in range(n):
        solved[n + r] = mm(inv_v[n + r], left[r]).astype(BF16)
    for copy in last_in:
        copy.wait()
    residual = leaf_residual(top_fac, solved, pattern, top - n, rhs_v[low])
    product = mm(both[...], residual)
    edge[...] = product[:block].astype(BF16)
    down[0] = (const[...] - product[block:]).astype(BF16)


def edge_call(pattern, link, rhs, inverse, factor, node_rhs, node_inverse, node_factor):
    n = LEVEL_ROWS
    coupled, block = factor.shape[1], factor.shape[2]
    loads = rhs.shape[-1]
    return pl.pallas_call(
        edge_kernel,
        out_shape=(
            pltpu.VMEM((2 * n, block, loads), BF16),
            pltpu.VMEM((block, loads), BF16),
            pltpu.VMEM((2, block, loads), BF16),
        ),
        in_specs=[HBM, SMEM] + [HBM] * 6,
        out_specs=(VMEM,) * 3,
        scratch_shapes=[
            pltpu.SMEM(pattern.shape, jnp.int32),
            pltpu.VMEM((2 * n + 1, block, loads), BF16),
            pltpu.VMEM((2 * n, block, block), BF16),
            pltpu.VMEM((n, coupled, block, block), BF16),
            pltpu.VMEM((coupled, block, block), BF16),
            pltpu.VMEM((n, block, loads), BF16),
            pltpu.VMEM((2 * block, block), BF16),
            pltpu.VMEM((block, loads), F32),
            pltpu.VMEM((block, loads), BF16),
            pltpu.VMEM((block, block), BF16),
            pltpu.VMEM((2, block, block), BF16),
            pltpu.SemaphoreType.DMA((12,)),
        ],
        compiler_params=pltpu.CompilerParams(vmem_limit_bytes=16 << 20),
        name="leaf_edge",
    )(
        in_hbm(pattern), link, in_hbm(rhs), in_hbm(inverse), in_hbm(factor),
        in_hbm(node_rhs), in_hbm(node_inverse), in_hbm(node_factor),
    )


def node_zero_kernel(down, lower, *rest):
    rest[-1][...] = (down[0].astype(F32) - mm(down[1], lower[...])).astype(BF16)


def level_one_kernel(inner, below, above, edge, lower_mat, upper_mat, const, out):
    odd = lax.rem(lax.axis_index("rows"), 2) == 1

    @pl.when(odd)
    def _():
        upper = (above[0].astype(F32) - mm(above[1], edge[...])).astype(BF16)
        total = const[0] - mm(lower_mat[0], inner[...]) - mm(upper_mat[0], upper)
        out[...] = total.astype(BF16)

    @pl.when(jnp.logical_not(odd))
    def _():
        total = const[0] - mm(upper_mat[0], inner[...]) - mm(lower_mat[0], below[...])
        out[...] = total.astype(BF16)


def small_call(kernel, name, shape, *args):
    return pl.pallas_call(
        kernel,
        out_shape=pltpu.VMEM(shape, BF16),
        in_specs=[VMEM] * len(args),
        out_specs=VMEM,
        compiler_params=pltpu.CompilerParams(vmem_limit_bytes=8 << 20),
        name=name,
    )(*args)


def rest_kernel(columns, rhs, inverse, factor, low, top, pattern, rhs_v, inv_v, fac_v, left, sem):
    n = LEVEL_ROWS

    def load(src, dst, slot):
        copy = pltpu.make_async_copy(src, dst, sem.at[slot])
        copy.start()
        return copy

    pattern_in = load(columns, pattern, 0)
    rhs_in = load(rhs.at[pl.ds(2 * n, n)], rhs_v, 1)
    fac_in = [load(factor.at[n + r], fac_v.at[r], 3 + r) for r in range(n)]
    inv_in = load(inverse.at[pl.ds(2 * n, n)], inv_v, 2)
    pattern_in.wait()
    rhs_in.wait()
    for r in range(n):
        fac_in[r].wait()
        left[r] = leaf_residual(fac_v.at[r], low, pattern, n + r, rhs_v[r])
    inv_in.wait()
    for r in range(n):
        top[r] = mm(inv_v[r], left[r]).astype(BF16)


def rest_call(pattern, rhs, inverse, factor, low):
    n = LEVEL_ROWS
    coupled, block = factor.shape[1], factor.shape[2]
    loads = rhs.shape[-1]
    flops = 2 * n * (coupled + 1) * block * block * loads
    return pl.pallas_call(
        rest_kernel,
        out_shape=pltpu.VMEM((n, block, loads), BF16),
        in_specs=[HBM] * 4 + [VMEM],
        out_specs=VMEM,
        scratch_shapes=[
            pltpu.SMEM(pattern.shape, jnp.int32),
            pltpu.VMEM((n, block, loads), BF16),
            pltpu.VMEM((n, block, block), BF16),
            pltpu.VMEM((n, coupled, block, block), BF16),
            pltpu.VMEM((n, block, loads), BF16),
            pltpu.SemaphoreType.DMA((3 + n,)),
        ],
        compiler_params=pltpu.CompilerParams(vmem_limit_bytes=12 << 20),
        cost_estimate=pl.CostEstimate(
            flops=flops, bytes_accessed=36 * block * block * 2, transcendentals=0
        ),
        name="leaf_rest",
    )(in_hbm(pattern), in_hbm(rhs), in_hbm(inverse), in_hbm(factor), low)


def fold_kernel(rhs, inverse, factor, _, lower_mat, upper_mat, const):
    for h in range(1, rhs.shape[0]):
        inv = inverse[h, 0]
        lower_mat[h - 1] = mm(inv, factor[h, 0, 0]).astype(BF16)
        upper_mat[h - 1] = mm(inv, factor[h, 0, 1]).astype(BF16)
        const[h - 1] = mm(inv, rhs[h, 0])


def fold_call(rhs, inverse, factor, after):
    depth, _, block, loads = rhs.shape
    depth = depth - 1
    return pl.pallas_call(
        fold_kernel,
        out_shape=(
            pltpu.VMEM((depth, block, block), BF16),
            pltpu.VMEM((depth, block, block), BF16),
            pltpu.VMEM((depth, block, loads), F32),
        ),
        in_specs=[VMEM] * 4,
        out_specs=(VMEM, VMEM, VMEM),
        cost_estimate=pl.CostEstimate(
            flops=6 * depth * block * block * loads,
            bytes_accessed=8 * depth * block * block * 2,
            transcendentals=0,
        ),
        compiler_params=pltpu.CompilerParams(vmem_limit_bytes=16 << 20),
        name="fold",
    )(rhs, inverse, factor, after)


def node_kernel(h, lower, upper, lower_mat, upper_mat, const, out):
    total = const[h] - mm(upper_mat[h], upper[...]) - mm(lower_mat[h], lower[...])
    out[...] = total.astype(BF16)


def collect_kernel(low, top, *refs):
    *levels, solved, out, sem = refs
    copies = [
        pltpu.make_async_copy(level, out.at[h, 0], sem.at[h]) for h, level in enumerate(levels)
    ]
    n = low.shape[0]
    h = len(levels)
    copies.append(pltpu.make_async_copy(low, solved.at[pl.ds(0, n)], sem.at[h]))
    copies.append(pltpu.make_async_copy(top, solved.at[pl.ds(n, top.shape[0])], sem.at[h + 1]))
    for copy in copies:
        copy.start()
    for copy in copies:
        copy.wait()


def collect_call(low, top, levels, shape):
    rows = low.shape[0] + top.shape[0]
    return pl.pallas_call(
        collect_kernel,
        out_shape=(
            jax.ShapeDtypeStruct((rows,) + low.shape[1:], BF16),
            jax.ShapeDtypeStruct(shape, BF16),
        ),
        in_specs=[VMEM] * (2 + len(levels)),
        out_specs=(HBM, HBM),
        scratch_shapes=[pltpu.SemaphoreType.DMA((2 + len(levels),))],
        compiler_params=pltpu.CompilerParams(vmem_limit_bytes=4 << 20),
        cost_estimate=pl.CostEstimate(
            flops=0,
            bytes_accessed=(rows + len(levels)) * shape[2] * shape[3] * 4,
            transcendentals=0,
        ),
        name="collect",
    )(low, top, *levels)


def last_kernel(lower, upper, lower_mat, upper_mat, const, _, out, piece, sem):
    h = const.shape[0] - 1
    rows = const.shape[1] // 2
    copies = []
    for half in range(2):
        part = pl.ds(half * rows, rows)
        total = (
            const[h, part]
            - mm(upper_mat[h, part], upper[...])
            - mm(lower_mat[h, part], lower[...])
        )
        piece[part] = total.astype(BF16)
        copy = pltpu.make_async_copy(
            piece.at[part], out.at[out.shape[0] - 1, 0, part], sem.at[half]
        )
        copy.start()
        copies.append(copy)
    for copy in copies:
        copy.wait()


def last_call(lower, upper, lower_mat, upper_mat, const, collected):
    return pl.pallas_call(
        last_kernel,
        out_shape=jax.ShapeDtypeStruct(collected.shape, BF16),
        in_specs=[VMEM] * 5 + [HBM],
        out_specs=HBM,
        input_output_aliases={5: 0},
        scratch_shapes=[pltpu.VMEM(lower.shape, BF16), pltpu.SemaphoreType.DMA((2,))],
        compiler_params=pltpu.CompilerParams(vmem_limit_bytes=8 << 20),
        name="node_last",
    )(lower, upper, lower_mat, upper_mat, const, collected)


def shards(
    leaf_rhs,
    separator_rhs,
    leaf_inverse,
    leaf_factor,
    separator_inverse,
    separator_factor,
    block_pattern,
    link_row,
):
    columns = block_pattern.T
    low, edge, down = edge_call(
        columns, link_row, leaf_rhs, leaf_inverse, leaf_factor,
        separator_rhs, separator_inverse, separator_factor,
    )
    shape = edge.shape
    edge_below = passed_along(edge, "rows", 1)
    edge_inner = pair_swap(edge, "rows")
    early = small_call(node_zero_kernel, "level0_early", shape, down, edge_inner)
    below = passed_along(early, "rows", 1)
    above = passed_along(down, "rows", -1)
    top = rest_call(columns, leaf_rhs, leaf_inverse, leaf_factor, low)
    mats = fold_call(separator_rhs, separator_inverse, separator_factor, early)
    block = small_call(
        node_zero_kernel, "level0_late", shape, down, edge_below, top, mats[2], below
    )
    inner = pair_swap(block, "rows")
    levels = [block]
    block = small_call(
        level_one_kernel, "level1", shape, inner, below, above, edge, *mats
    )
    levels.append(block)
    depth = separator_rhs.shape[0]
    for height in range(2, depth):
        stride = 2 ** (height - 1)
        lower = passed_along(block, "rows", stride)
        upper = passed_along(block, "rows", -stride)
        if height < depth - 1:
            step = functools.partial(node_kernel, height - 1)
            block = small_call(step, f"level{height}", shape, lower, upper, *mats)
            levels.append(block)
    solved, collected = collect_call(low, top, levels, (depth, 1) + shape)
    return solved, last_call(lower, upper, *mats, collected)


def solution(mesh):
    placed = (
        P("rows", None, None),
        P(None, "rows", None, None),
        P(("draws", "rows"), None, None),
        P(("draws", "rows"), None, None, None),
        P(None, ("draws", "rows"), None, None),
        P(None, ("draws", "rows"), None, None, None),
        P("rows", None),
        P("rows"),
    )
    return jax.shard_map(
        shards,
        mesh=mesh,
        in_specs=placed,
        out_specs=(P(("draws", "rows"), None, None), P(None, ("draws", "rows"), None, None)),
        check_vma=False,
    )
```

```python
import functools

import jax
import jax.numpy as jnp
from jax import lax
from jax.experimental import pallas as pl
from jax.experimental.pallas import tpu as pltpu
from jax.sharding import PartitionSpec as P

LEVEL_ROWS = 4
LEAF_LEVELS = 3
F32 = jnp.float32
BF16 = jnp.bfloat16

SMEM = pl.BlockSpec(memory_space=pltpu.SMEM)
VMEM = pl.BlockSpec(memory_space=pltpu.VMEM)
HBM = pl.BlockSpec(memory_space=pltpu.HBM)


def passed_along(value, axis, by):
    length = lax.axis_size(axis)
    return lax.ppermute(value, axis, [(i, (i + by) % length) for i in range(length)])


def in_hbm(array):
    return pltpu.with_memory_space_constraint(array, pltpu.HBM)


def mm(a, b):
    return jnp.dot(a, b, preferred_element_type=F32)


def leaf_residual(factor, solved, pattern, row, rhs):
    coupled = factor.shape[0]
    wide = jnp.concatenate([factor[k] for k in range(coupled)], axis=1)
    tall = jnp.concatenate([solved[pattern[k, row]] for k in range(coupled)], axis=0)
    return (rhs.astype(F32) - mm(wide, tall)).astype(BF16)


def pair_swap(value, axis):
    length = lax.axis_size(axis)
    return lax.ppermute(value, axis, [(i, i ^ 1) for i in range(length)])


def edge_kernel(
    columns, link, rhs, inverse, factor, node_rhs, node_inverse, node_factor,
    solved, edge, down, lower_mat,
    pattern, rhs_v, inv_v, fac_v, top_fac, left, both, const, node_r, node_i, node_f, sem,
):
    n = LEVEL_ROWS
    low = 2 * n
    block = factor.shape[2]
    slots = iter(range(sem.shape[0]))

    def load(src, dst):
        copy = pltpu.make_async_copy(src, dst, sem.at[next(slots)])
        copy.start()
        return copy

    top = link[0]
    first_in = (
        load(inverse.at[pl.ds(0, n)], inv_v.at[pl.ds(0, n)]),
        load(rhs.at[pl.ds(0, n)], rhs_v.at[pl.ds(0, n)]),
    )
    node_in = (
        load(node_inverse.at[0, 0], node_i),
        load(node_factor.at[0, 0], node_f),
        load(node_rhs.at[0, 0], node_r),
        load(inverse.at[top], both.at[pl.ds(0, block)]),
    )
    next_in = (
        load(columns, pattern),
        load(rhs.at[pl.ds(n, n)], rhs_v.at[pl.ds(n, n)]),
        load(inverse.at[pl.ds(n, n)], inv_v.at[pl.ds(n, n)]),
        load(factor.at[pl.ds(0, n)], fac_v),
    )
    last_in = (
        load(rhs.at[top], rhs_v.at[low]),
        load(factor.at[top - n], top_fac),
    )
    for copy in first_in:
        copy.wait()
    for r in range(n):
        solved[r] = mm(inv_v[r], rhs_v[r]).astype(BF16)
    for copy in node_in:
        copy.wait()
    lower_mat[...] = mm(node_i[...], node_f[0]).astype(BF16)
    upper = mm(node_i[...], node_f[1]).astype(BF16)
    const[...] = mm(node_i[...], node_r[...])
    both[pl.ds(block, block)] = mm(upper, both[pl.ds(0, block)]).astype(BF16)
    for copy in next_in:
        copy.wait()
    for r in range(n):
        left[r] = leaf_residual(fac_v.at[r], solved, pattern, r, rhs_v[n + r])
    for r in range(n):
        solved[n + r] = mm(inv_v[n + r], left[r]).astype(BF16)
    for copy in last_in:
        copy.wait()
    residual = leaf_residual(top_fac, solved, pattern, top - n, rhs_v[low])
    product = mm(both[...], residual)
    edge[...] = product[:block].astype(BF16)
    down[...] = (const[...] - product[block:]).astype(BF16)


def edge_call(pattern, link, rhs, inverse, factor, node_rhs, node_inverse, node_factor):
    n = LEVEL_ROWS
    coupled, block = factor.shape[1], factor.shape[2]
    loads = rhs.shape[-1]
    return pl.pallas_call(
        edge_kernel,
        out_shape=(
            pltpu.VMEM((2 * n, block, loads), BF16),
            pltpu.VMEM((block, loads), BF16),
            pltpu.VMEM((block, loads), BF16),
            pltpu.VMEM((block, block), BF16),
        ),
        in_specs=[HBM, SMEM] + [HBM] * 6,
        out_specs=(VMEM,) * 4,
        scratch_shapes=[
            pltpu.SMEM(pattern.shape, jnp.int32),
            pltpu.VMEM((2 * n + 1, block, loads), BF16),
            pltpu.VMEM((2 * n, block, block), BF16),
            pltpu.VMEM((n, coupled, block, block), BF16),
            pltpu.VMEM((coupled, block, block), BF16),
            pltpu.VMEM((n, block, loads), BF16),
            pltpu.VMEM((2 * block, block), BF16),
            pltpu.VMEM((block, loads), F32),
            pltpu.VMEM((block, loads), BF16),
            pltpu.VMEM((block, block), BF16),
            pltpu.VMEM((2, block, block), BF16),
            pltpu.SemaphoreType.DMA((12,)),
        ],
        compiler_params=pltpu.CompilerParams(vmem_limit_bytes=16 << 20),
        name="leaf_edge",
    )(
        in_hbm(pattern), link, in_hbm(rhs), in_hbm(inverse), in_hbm(factor),
        in_hbm(node_rhs), in_hbm(node_inverse), in_hbm(node_factor),
    )


def node_zero_kernel(down, lower_mat, lower, *rest):
    rest[-1][...] = (down[...].astype(F32) - mm(lower_mat[...], lower[...])).astype(BF16)


def below_kernel(below, lower_mat, const, out):
    odd = lax.rem(lax.axis_index("rows"), 2) == 1

    @pl.when(odd)
    def _():
        out[...] = const[0]

    @pl.when(jnp.logical_not(odd))
    def _():
        out[...] = const[0] - mm(lower_mat[0], below[...])


def across_kernel(part, above, above_mat, edge, upper_mat, out):
    odd = lax.rem(lax.axis_index("rows"), 2) == 1

    @pl.when(odd)
    def _():
        upper = (above[...].astype(F32) - mm(above_mat[...], edge[...])).astype(BF16)
        out[...] = part[...] - mm(upper_mat[0], upper)

    @pl.when(jnp.logical_not(odd))
    def _():
        out[...] = part[...]


def level_one_kernel(inner, part, lower_mat, upper_mat, out):
    odd = lax.rem(lax.axis_index("rows"), 2) == 1

    @pl.when(odd)
    def _():
        out[...] = (part[...] - mm(lower_mat[0], inner[...])).astype(BF16)

    @pl.when(jnp.logical_not(odd))
    def _():
        out[...] = (part[...] - mm(upper_mat[0], inner[...])).astype(BF16)


def small_call(kernel, name, shape, *args, dtype=BF16):
    return pl.pallas_call(
        kernel,
        out_shape=pltpu.VMEM(shape, dtype),
        in_specs=[VMEM] * len(args),
        out_specs=VMEM,
        compiler_params=pltpu.CompilerParams(vmem_limit_bytes=8 << 20),
        name=name,
    )(*args)


def rest_kernel(columns, rhs, inverse, factor, low, _, top, pattern, rhs_v, inv_v, fac_v, left, sem):
    n = LEVEL_ROWS

    def load(src, dst, slot):
        copy = pltpu.make_async_copy(src, dst, sem.at[slot])
        copy.start()
        return copy

    pattern_in = load(columns, pattern, 0)
    rhs_in = load(rhs.at[pl.ds(2 * n, n)], rhs_v, 1)
    fac_in = [load(factor.at[n + r], fac_v.at[r], 3 + r) for r in range(n)]
    inv_in = load(inverse.at[pl.ds(2 * n, n)], inv_v, 2)
    pattern_in.wait()
    rhs_in.wait()
    for r in range(n):
        fac_in[r].wait()
        left[r] = leaf_residual(fac_v.at[r], low, pattern, n + r, rhs_v[r])
    inv_in.wait()
    for r in range(n):
        top[r] = mm(inv_v[r], left[r]).astype(BF16)


def rest_call(pattern, rhs, inverse, factor, low, after):
    n = LEVEL_ROWS
    coupled, block = factor.shape[1], factor.shape[2]
    loads = rhs.shape[-1]
    flops = 2 * n * (coupled + 1) * block * block * loads
    return pl.pallas_call(
        rest_kernel,
        out_shape=pltpu.VMEM((n, block, loads), BF16),
        in_specs=[HBM] * 4 + [VMEM] * 2,
        out_specs=VMEM,
        scratch_shapes=[
            pltpu.SMEM(pattern.shape, jnp.int32),
            pltpu.VMEM((n, block, loads), BF16),
            pltpu.VMEM((n, block, block), BF16),
            pltpu.VMEM((n, coupled, block, block), BF16),
            pltpu.VMEM((n, block, loads), BF16),
            pltpu.SemaphoreType.DMA((3 + n,)),
        ],
        compiler_params=pltpu.CompilerParams(vmem_limit_bytes=12 << 20),
        cost_estimate=pl.CostEstimate(
            flops=flops, bytes_accessed=36 * block * block * 2, transcendentals=0
        ),
        name="leaf_rest",
    )(in_hbm(pattern), in_hbm(rhs), in_hbm(inverse), in_hbm(factor), low, after)


def fold_kernel(rhs, inverse, factor, _, lower_mat, upper_mat, const):
    for h in range(1, rhs.shape[0]):
        inv = inverse[h, 0]
        lower_mat[h - 1] = mm(inv, factor[h, 0, 0]).astype(BF16)
        upper_mat[h - 1] = mm(inv, factor[h, 0, 1]).astype(BF16)
        const[h - 1] = mm(inv, rhs[h, 0])


def fold_call(rhs, inverse, factor, after):
    depth, _, block, loads = rhs.shape
    depth = depth - 1
    return pl.pallas_call(
        fold_kernel,
        out_shape=(
            pltpu.VMEM((depth, block, block), BF16),
            pltpu.VMEM((depth, block, block), BF16),
            pltpu.VMEM((depth, block, loads), F32),
        ),
        in_specs=[VMEM] * 4,
        out_specs=(VMEM, VMEM, VMEM),
        cost_estimate=pl.CostEstimate(
            flops=6 * depth * block * block * loads,
            bytes_accessed=8 * depth * block * block * 2,
            transcendentals=0,
        ),
        compiler_params=pltpu.CompilerParams(vmem_limit_bytes=16 << 20),
        name="fold",
    )(rhs, inverse, factor, after)


def node_kernel(h, lower, upper, lower_mat, upper_mat, const, *rest):
    total = const[h] - mm(upper_mat[h], upper[...]) - mm(lower_mat[h], lower[...])
    rest[-1][...] = total.astype(BF16)


def collect_kernel(low, top, *refs):
    *levels, solved, out, sem = refs
    copies = [
        pltpu.make_async_copy(level, out.at[h, 0], sem.at[h]) for h, level in enumerate(levels)
    ]
    n = low.shape[0]
    h = len(levels)
    copies.append(pltpu.make_async_copy(low, solved.at[pl.ds(0, n)], sem.at[h]))
    copies.append(pltpu.make_async_copy(top, solved.at[pl.ds(n, top.shape[0])], sem.at[h + 1]))
    for copy in copies:
        copy.start()
    for copy in copies:
        copy.wait()


def collect_call(low, top, levels, shape):
    rows = low.shape[0] + top.shape[0]
    return pl.pallas_call(
        collect_kernel,
        out_shape=(
            jax.ShapeDtypeStruct((rows,) + low.shape[1:], BF16),
            jax.ShapeDtypeStruct(shape, BF16),
        ),
        in_specs=[VMEM] * (2 + len(levels)),
        out_specs=(HBM, HBM),
        scratch_shapes=[pltpu.SemaphoreType.DMA((2 + len(levels),))],
        compiler_params=pltpu.CompilerParams(vmem_limit_bytes=4 << 20),
        cost_estimate=pl.CostEstimate(
            flops=0,
            bytes_accessed=(rows + len(levels)) * shape[2] * shape[3] * 4,
            transcendentals=0,
        ),
        name="collect",
    )(low, top, *levels)


def last_kernel(lower, upper, lower_mat, upper_mat, const, _, out, piece, sem):
    h = const.shape[0] - 1
    rows = const.shape[1] // 2
    copies = []
    for half in range(2):
        part = pl.ds(half * rows, rows)
        total = (
            const[h, part]
            - mm(upper_mat[h, part], upper[...])
            - mm(lower_mat[h, part], lower[...])
        )
        piece[part] = total.astype(BF16)
        copy = pltpu.make_async_copy(
            piece.at[part], out.at[out.shape[0] - 1, 0, part], sem.at[half]
        )
        copy.start()
        copies.append(copy)
    for copy in copies:
        copy.wait()


def last_call(lower, upper, lower_mat, upper_mat, const, collected):
    return pl.pallas_call(
        last_kernel,
        out_shape=jax.ShapeDtypeStruct(collected.shape, BF16),
        in_specs=[VMEM] * 5 + [HBM],
        out_specs=HBM,
        input_output_aliases={5: 0},
        scratch_shapes=[pltpu.VMEM(lower.shape, BF16), pltpu.SemaphoreType.DMA((2,))],
        compiler_params=pltpu.CompilerParams(vmem_limit_bytes=8 << 20),
        name="node_last",
    )(lower, upper, lower_mat, upper_mat, const, collected)


def shards(
    leaf_rhs,
    separator_rhs,
    leaf_inverse,
    leaf_factor,
    separator_inverse,
    separator_factor,
    block_pattern,
    link_row,
):
    columns = block_pattern.T
    low, edge, down, lower_zero = edge_call(
        columns, link_row, leaf_rhs, leaf_inverse, leaf_factor,
        separator_rhs, separator_inverse, separator_factor,
    )
    shape = edge.shape
    edge_below = passed_along(edge, "rows", 1)
    edge_inner = pair_swap(edge, "rows")
    early = small_call(node_zero_kernel, "level0_early", shape, down, lower_zero, edge_inner)
    below = passed_along(early, "rows", 1)
    above = passed_along(down, "rows", -1)
    above_mat = passed_along(lower_zero, "rows", -1)
    mats = fold_call(separator_rhs, separator_inverse, separator_factor, early)
    block = small_call(
        node_zero_kernel, "level0_late", shape, down, lower_zero, edge_below
    )
    inner = pair_swap(block, "rows")
    levels = [block]
    part = small_call(
        below_kernel, "level1_below", shape, below, mats[0], mats[2], dtype=F32
    )
    part = small_call(
        across_kernel, "level1_across", shape, part, above, above_mat, edge, mats[1],
        dtype=F32,
    )
    block = small_call(level_one_kernel, "level1", shape, inner, part, *mats[:2])
    top = rest_call(columns, leaf_rhs, leaf_inverse, leaf_factor, low, block)
    levels.append(block)
    depth = separator_rhs.shape[0]
    for height in range(2, depth):
        stride = 2 ** (height - 1)
        lower = passed_along(block, "rows", stride)
        upper = passed_along(block, "rows", -stride)
        if height < depth - 1:
            step = functools.partial(node_kernel, height - 1)
            block = small_call(step, f"level{height}", shape, lower, upper, *mats, top)
            levels.append(block)
    solved, collected = collect_call(low, top, levels, (depth, 1) + shape)
    return solved, last_call(lower, upper, *mats, collected)


def solution(mesh):
    placed = (
        P("rows", None, None),
        P(None, "rows", None, None),
        P(("draws", "rows"), None, None),
        P(("draws", "rows"), None, None, None),
        P(None, ("draws", "rows"), None, None),
        P(None, ("draws", "rows"), None, None, None),
        P("rows", None),
        P("rows"),
    )
    return jax.shard_map(
        shards,
        mesh=mesh,
        in_specs=placed,
        out_specs=(P(("draws", "rows"), None, None), P(None, ("draws", "rows"), None, None)),
        check_vma=False,
    )
```

```python
import functools

import jax
import jax.numpy as jnp
from jax import lax
from jax.experimental import pallas as pl
from jax.experimental.pallas import tpu as pltpu
from jax.sharding import PartitionSpec as P

LEVEL_ROWS = 4
LEAF_LEVELS = 3
F32 = jnp.float32
BF16 = jnp.bfloat16

SMEM = pl.BlockSpec(memory_space=pltpu.SMEM)
VMEM = pl.BlockSpec(memory_space=pltpu.VMEM)
HBM = pl.BlockSpec(memory_space=pltpu.HBM)


def passed_along(value, axis, by):
    length = lax.axis_size(axis)
    return lax.ppermute(value, axis, [(i, (i + by) % length) for i in range(length)])


def in_hbm(array):
    return pltpu.with_memory_space_constraint(array, pltpu.HBM)


def edge_swap(value, axis, stride, odd):
    length = lax.axis_size(axis)
    pairs = []
    for i in range(length):
        step = stride if (i // stride % 2 == 0) != odd else -stride
        pairs.append((i, (i + step) % length))
    return lax.ppermute(value, axis, pairs)


def stride_bit(stride):
    return lax.rem(lax.div(lax.axis_index("rows"), stride), 2)


def mm(a, b):
    return jnp.dot(a, b, preferred_element_type=F32)


def leaf_residual(factor, solved, pattern, row, rhs):
    coupled = factor.shape[0]
    wide = jnp.concatenate([factor[k] for k in range(coupled)], axis=1)
    tall = jnp.concatenate([solved[pattern[k, row]] for k in range(coupled)], axis=0)
    return (rhs.astype(F32) - mm(wide, tall)).astype(BF16)


def pair_swap(value, axis):
    length = lax.axis_size(axis)
    return lax.ppermute(value, axis, [(i, i ^ 1) for i in range(length)])


def edge_kernel(
    columns, link, rhs, inverse, factor, node_rhs, node_inverse, node_factor,
    solved, edge, down, lower_mat,
    pattern, rhs_v, inv_v, fac_v, top_fac, left, both, const, node_r, node_i, node_f, sem,
):
    n = LEVEL_ROWS
    low = 2 * n
    block = factor.shape[2]
    slots = iter(range(sem.shape[0]))

    def load(src, dst):
        copy = pltpu.make_async_copy(src, dst, sem.at[next(slots)])
        copy.start()
        return copy

    top = link[0]
    first_in = (
        load(inverse.at[pl.ds(0, n)], inv_v.at[pl.ds(0, n)]),
        load(rhs.at[pl.ds(0, n)], rhs_v.at[pl.ds(0, n)]),
    )
    node_in = (
        load(node_inverse.at[0, 0], node_i),
        load(node_factor.at[0, 0], node_f),
        load(node_rhs.at[0, 0], node_r),
        load(inverse.at[top], both.at[pl.ds(0, block)]),
    )
    next_in = (
        load(columns, pattern),
        load(rhs.at[pl.ds(n, n)], rhs_v.at[pl.ds(n, n)]),
        load(inverse.at[pl.ds(n, n)], inv_v.at[pl.ds(n, n)]),
        load(factor.at[pl.ds(0, n)], fac_v),
    )
    last_in = (
        load(rhs.at[top], rhs_v.at[low]),
        load(factor.at[top - n], top_fac),
    )
    for copy in first_in:
        copy.wait()
    for r in range(n):
        solved[r] = mm(inv_v[r], rhs_v[r]).astype(BF16)
    for copy in node_in:
        copy.wait()
    lower_mat[...] = mm(node_i[...], node_f[0]).astype(BF16)
    upper = mm(node_i[...], node_f[1]).astype(BF16)
    const[...] = mm(node_i[...], node_r[...])
    both[pl.ds(block, block)] = mm(upper, both[pl.ds(0, block)]).astype(BF16)
    for copy in next_in:
        copy.wait()
    for r in range(n):
        left[r] = leaf_residual(fac_v.at[r], solved, pattern, r, rhs_v[n + r])
    for r in range(n):
        solved[n + r] = mm(inv_v[n + r], left[r]).astype(BF16)
    for copy in last_in:
        copy.wait()
    residual = leaf_residual(top_fac, solved, pattern, top - n, rhs_v[low])
    product = mm(both[...], residual)
    edge[...] = product[:block].astype(BF16)
    down[...] = (const[...] - product[block:]).astype(BF16)


def edge_call(pattern, link, rhs, inverse, factor, node_rhs, node_inverse, node_factor):
    n = LEVEL_ROWS
    coupled, block = factor.shape[1], factor.shape[2]
    loads = rhs.shape[-1]
    return pl.pallas_call(
        edge_kernel,
        out_shape=(
            pltpu.VMEM((2 * n, block, loads), BF16),
            pltpu.VMEM((block, loads), BF16),
            pltpu.VMEM((block, loads), BF16),
            pltpu.VMEM((block, block), BF16),
        ),
        in_specs=[HBM, SMEM] + [HBM] * 6,
        out_specs=(VMEM,) * 4,
        scratch_shapes=[
            pltpu.SMEM(pattern.shape, jnp.int32),
            pltpu.VMEM((2 * n + 1, block, loads), BF16),
            pltpu.VMEM((2 * n, block, block), BF16),
            pltpu.VMEM((n, coupled, block, block), BF16),
            pltpu.VMEM((coupled, block, block), BF16),
            pltpu.VMEM((n, block, loads), BF16),
            pltpu.VMEM((2 * block, block), BF16),
            pltpu.VMEM((block, loads), F32),
            pltpu.VMEM((block, loads), BF16),
            pltpu.VMEM((block, block), BF16),
            pltpu.VMEM((2, block, block), BF16),
            pltpu.SemaphoreType.DMA((12,)),
        ],
        compiler_params=pltpu.CompilerParams(vmem_limit_bytes=16 << 20),
        name="leaf_edge",
    )(
        in_hbm(pattern), link, in_hbm(rhs), in_hbm(inverse), in_hbm(factor),
        in_hbm(node_rhs), in_hbm(node_inverse), in_hbm(node_factor),
    )


def node_zero_kernel(down, lower_mat, lower, *rest):
    rest[-1][...] = (down[...].astype(F32) - mm(lower_mat[...], lower[...])).astype(BF16)


def below_kernel(below, lower_mat, const, out):
    odd = lax.rem(lax.axis_index("rows"), 2) == 1

    @pl.when(odd)
    def _():
        out[...] = const[0]

    @pl.when(jnp.logical_not(odd))
    def _():
        out[...] = const[0] - mm(lower_mat[0], below[...])


def across_kernel(part, above, above_mat, edge, upper_mat, out):
    odd = lax.rem(lax.axis_index("rows"), 2) == 1

    @pl.when(odd)
    def _():
        upper = (above[...].astype(F32) - mm(above_mat[...], edge[...])).astype(BF16)
        out[...] = part[...] - mm(upper_mat[0], upper)

    @pl.when(jnp.logical_not(odd))
    def _():
        out[...] = part[...]


def level_one_kernel(inner, part, lower_mat, upper_mat, out):
    odd = lax.rem(lax.axis_index("rows"), 2) == 1

    @pl.when(odd)
    def _():
        out[...] = (part[...] - mm(lower_mat[0], inner[...])).astype(BF16)

    @pl.when(jnp.logical_not(odd))
    def _():
        out[...] = (part[...] - mm(upper_mat[0], inner[...])).astype(BF16)


def small_call(kernel, name, shape, *args, dtype=BF16):
    return pl.pallas_call(
        kernel,
        out_shape=pltpu.VMEM(shape, dtype),
        in_specs=[VMEM] * len(args),
        out_specs=VMEM,
        compiler_params=pltpu.CompilerParams(vmem_limit_bytes=8 << 20),
        name=name,
    )(*args)


def rest_kernel(columns, rhs, inverse, factor, low, _, top, pattern, rhs_v, inv_v, fac_v, left, sem):
    n = LEVEL_ROWS

    def load(src, dst, slot):
        copy = pltpu.make_async_copy(src, dst, sem.at[slot])
        copy.start()
        return copy

    pattern_in = load(columns, pattern, 0)
    rhs_in = load(rhs.at[pl.ds(2 * n, n)], rhs_v, 1)
    fac_in = [load(factor.at[n + r], fac_v.at[r], 3 + r) for r in range(n)]
    inv_in = load(inverse.at[pl.ds(2 * n, n)], inv_v, 2)
    pattern_in.wait()
    rhs_in.wait()
    for r in range(n):
        fac_in[r].wait()
        left[r] = leaf_residual(fac_v.at[r], low, pattern, n + r, rhs_v[r])
    inv_in.wait()
    for r in range(n):
        top[r] = mm(inv_v[r], left[r]).astype(BF16)


def rest_call(pattern, rhs, inverse, factor, low, after):
    n = LEVEL_ROWS
    coupled, block = factor.shape[1], factor.shape[2]
    loads = rhs.shape[-1]
    flops = 2 * n * (coupled + 1) * block * block * loads
    return pl.pallas_call(
        rest_kernel,
        out_shape=pltpu.VMEM((n, block, loads), BF16),
        in_specs=[HBM] * 4 + [VMEM] * 2,
        out_specs=VMEM,
        scratch_shapes=[
            pltpu.SMEM(pattern.shape, jnp.int32),
            pltpu.VMEM((n, block, loads), BF16),
            pltpu.VMEM((n, block, block), BF16),
            pltpu.VMEM((n, coupled, block, block), BF16),
            pltpu.VMEM((n, block, loads), BF16),
            pltpu.SemaphoreType.DMA((3 + n,)),
        ],
        compiler_params=pltpu.CompilerParams(vmem_limit_bytes=12 << 20),
        cost_estimate=pl.CostEstimate(
            flops=flops, bytes_accessed=36 * block * block * 2, transcendentals=0
        ),
        name="leaf_rest",
    )(in_hbm(pattern), in_hbm(rhs), in_hbm(inverse), in_hbm(factor), low, after)


def fold_kernel(rhs, inverse, factor, _, lower_mat, upper_mat, const):
    for h in range(1, rhs.shape[0]):
        inv = inverse[h, 0]
        lower_mat[h - 1] = mm(inv, factor[h, 0, 0]).astype(BF16)
        upper_mat[h - 1] = mm(inv, factor[h, 0, 1]).astype(BF16)
        const[h - 1] = mm(inv, rhs[h, 0])


def fold_call(rhs, inverse, factor, after):
    depth, _, block, loads = rhs.shape
    depth = depth - 1
    return pl.pallas_call(
        fold_kernel,
        out_shape=(
            pltpu.VMEM((depth, block, block), BF16),
            pltpu.VMEM((depth, block, block), BF16),
            pltpu.VMEM((depth, block, loads), F32),
        ),
        in_specs=[VMEM] * 4,
        out_specs=(VMEM, VMEM, VMEM),
        cost_estimate=pl.CostEstimate(
            flops=6 * depth * block * block * loads,
            bytes_accessed=8 * depth * block * block * 2,
            transcendentals=0,
        ),
        compiler_params=pltpu.CompilerParams(vmem_limit_bytes=16 << 20),
        name="fold",
    )(rhs, inverse, factor, after)


def node_total(h, rows, first, second, lower_mat, upper_mat, const, out, stride, swapped):
    def total(first_mat, second_mat):
        value = const[h, rows] - mm(first_mat[h, rows], first[...])
        out[rows] = (value - mm(second_mat[h, rows], second[...])).astype(BF16)

    if swapped is None:
        total(upper_mat, lower_mat)
        return
    if not swapped:
        total(lower_mat, upper_mat)
        return
    bit = stride_bit(stride)
    pl.when(bit == 1)(lambda: total(lower_mat, upper_mat))
    pl.when(bit == 0)(lambda: total(upper_mat, lower_mat))


def node_kernel(
    h, stride, swapped, first, second, lower_mat, upper_mat, const, *rest
):
    rows = pl.ds(0, const.shape[1])
    node_total(
        h, rows, first, second, lower_mat, upper_mat, const, rest[-1], stride, swapped
    )


def collect_kernel(low, top, *refs):
    *levels, solved, out, sem = refs
    copies = [
        pltpu.make_async_copy(level, out.at[h, 0], sem.at[h]) for h, level in enumerate(levels)
    ]
    n = low.shape[0]
    h = len(levels)
    copies.append(pltpu.make_async_copy(low, solved.at[pl.ds(0, n)], sem.at[h]))
    copies.append(pltpu.make_async_copy(top, solved.at[pl.ds(n, top.shape[0])], sem.at[h + 1]))
    for copy in copies:
        copy.start()
    for copy in copies:
        copy.wait()


def collect_call(low, top, levels, shape):
    rows = low.shape[0] + top.shape[0]
    return pl.pallas_call(
        collect_kernel,
        out_shape=(
            jax.ShapeDtypeStruct((rows,) + low.shape[1:], BF16),
            jax.ShapeDtypeStruct(shape, BF16),
        ),
        in_specs=[VMEM] * (2 + len(levels)),
        out_specs=(HBM, HBM),
        scratch_shapes=[pltpu.SemaphoreType.DMA((2 + len(levels),))],
        compiler_params=pltpu.CompilerParams(vmem_limit_bytes=4 << 20),
        cost_estimate=pl.CostEstimate(
            flops=0,
            bytes_accessed=(rows + len(levels)) * shape[2] * shape[3] * 4,
            transcendentals=0,
        ),
        name="collect",
    )(low, top, *levels)


def last_kernel(
    stride, swapped, first, second, lower_mat, upper_mat, const, _, out, piece, sem
):
    h = const.shape[0] - 1
    size = const.shape[1] // 2
    copies = []
    for half in range(2):
        rows = pl.ds(half * size, size)
        node_total(
            h, rows, first, second, lower_mat, upper_mat, const, piece, stride, swapped
        )
        copy = pltpu.make_async_copy(
            piece.at[rows], out.at[out.shape[0] - 1, 0, rows], sem.at[half]
        )
        copy.start()
        copies.append(copy)
    for copy in copies:
        copy.wait()


def last_call(stride, swapped, first, second, lower_mat, upper_mat, const, collected):
    return pl.pallas_call(
        functools.partial(last_kernel, stride, swapped),
        out_shape=jax.ShapeDtypeStruct(collected.shape, BF16),
        in_specs=[VMEM] * 5 + [HBM],
        out_specs=HBM,
        input_output_aliases={5: 0},
        scratch_shapes=[pltpu.VMEM(first.shape, BF16), pltpu.SemaphoreType.DMA((2,))],
        compiler_params=pltpu.CompilerParams(vmem_limit_bytes=8 << 20),
        name="node_last",
    )(first, second, lower_mat, upper_mat, const, collected)


def shards(
    leaf_rhs,
    separator_rhs,
    leaf_inverse,
    leaf_factor,
    separator_inverse,
    separator_factor,
    block_pattern,
    link_row,
):
    columns = block_pattern.T
    low, edge, down, lower_zero = edge_call(
        columns, link_row, leaf_rhs, leaf_inverse, leaf_factor,
        separator_rhs, separator_inverse, separator_factor,
    )
    shape = edge.shape
    edge_below = passed_along(edge, "rows", 1)
    edge_inner = pair_swap(edge, "rows")
    early = small_call(node_zero_kernel, "level0_early", shape, down, lower_zero, edge_inner)
    below = passed_along(early, "rows", 1)
    above = passed_along(down, "rows", -1)
    above_mat = passed_along(lower_zero, "rows", -1)
    mats = fold_call(separator_rhs, separator_inverse, separator_factor, early)
    block = small_call(
        node_zero_kernel, "level0_late", shape, down, lower_zero, edge_below
    )
    inner = pair_swap(block, "rows")
    levels = [block]
    part = small_call(
        below_kernel, "level1_below", shape, below, mats[0], mats[2], dtype=F32
    )
    part = small_call(
        across_kernel, "level1_across", shape, part, above, above_mat, edge, mats[1],
        dtype=F32,
    )
    block = small_call(level_one_kernel, "level1", shape, inner, part, *mats[:2])
    top = rest_call(columns, leaf_rhs, leaf_inverse, leaf_factor, low, block)
    levels.append(block)
    depth = separator_rhs.shape[0]
    for height in range(2, depth):
        stride = 2 ** (height - 1)
        last = height == depth - 1
        swapped = not last
        if swapped:
            first = edge_swap(block, "rows", stride, False)
            second = edge_swap(block, "rows", stride, True)
        else:
            first = passed_along(block, "rows", -stride)
            second = passed_along(block, "rows", stride)
        if not swapped:
            swapped = None
        if not last:
            step = functools.partial(node_kernel, height - 1, stride, swapped)
            block = small_call(step, f"level{height}", shape, first, second, *mats, top)
            levels.append(block)
    solved, collected = collect_call(low, top, levels, (depth, 1) + shape)
    return solved, last_call(stride, swapped, first, second, *mats, collected)


def solution(mesh):
    placed = (
        P("rows", None, None),
        P(None, "rows", None, None),
        P(("draws", "rows"), None, None),
        P(("draws", "rows"), None, None, None),
        P(None, ("draws", "rows"), None, None),
        P(None, ("draws", "rows"), None, None, None),
        P("rows", None),
        P("rows"),
    )
    return jax.shard_map(
        shards,
        mesh=mesh,
        in_specs=placed,
        out_specs=(P(("draws", "rows"), None, None), P(None, ("draws", "rows"), None, None)),
        check_vma=False,
    )
```

```python
import functools

import jax
import jax.numpy as jnp
from jax import lax
from jax.experimental import pallas as pl
from jax.experimental.pallas import tpu as pltpu
from jax.sharding import PartitionSpec as P

LEVEL_ROWS = 4
LEAF_LEVELS = 3
F32 = jnp.float32
BF16 = jnp.bfloat16

SMEM = pl.BlockSpec(memory_space=pltpu.SMEM)
VMEM = pl.BlockSpec(memory_space=pltpu.VMEM)
HBM = pl.BlockSpec(memory_space=pltpu.HBM)


def passed_along(value, axis, by):
    length = lax.axis_size(axis)
    return lax.ppermute(value, axis, [(i, (i + by) % length) for i in range(length)])


def in_hbm(array):
    return pltpu.with_memory_space_constraint(array, pltpu.HBM)


def edge_swap(value, axis, stride, odd):
    length = lax.axis_size(axis)
    pairs = []
    for i in range(length):
        step = stride if (i // stride % 2 == 0) != odd else -stride
        pairs.append((i, (i + step) % length))
    return lax.ppermute(value, axis, pairs)


def stride_bit(stride):
    return lax.rem(lax.div(lax.axis_index("rows"), stride), 2)


def mm(a, b):
    return jnp.dot(a, b, preferred_element_type=F32)


def leaf_residual(factor, solved, pattern, row, rhs):
    coupled = factor.shape[0]
    wide = jnp.concatenate([factor[k] for k in range(coupled)], axis=1)
    tall = jnp.concatenate([solved[pattern[k, row]] for k in range(coupled)], axis=0)
    return (rhs.astype(F32) - mm(wide, tall)).astype(BF16)


def pair_swap(value, axis):
    length = lax.axis_size(axis)
    return lax.ppermute(value, axis, [(i, i ^ 1) for i in range(length)])


def edge_kernel(
    columns, link, rhs, inverse, factor, node_rhs, node_inverse, node_factor,
    solved, edge, down, lower_mat,
    pattern, rhs_v, inv_v, fac_v, top_fac, left, both, const, node_r, node_i, node_f, sem,
):
    n = LEVEL_ROWS
    low = 2 * n
    block = factor.shape[2]
    slots = iter(range(sem.shape[0]))

    def load(src, dst):
        copy = pltpu.make_async_copy(src, dst, sem.at[next(slots)])
        copy.start()
        return copy

    top = link[0]
    first_in = (
        load(inverse.at[pl.ds(0, n)], inv_v.at[pl.ds(0, n)]),
        load(rhs.at[pl.ds(0, n)], rhs_v.at[pl.ds(0, n)]),
    )
    node_in = (
        load(node_inverse.at[0, 0], node_i),
        load(node_factor.at[0, 0], node_f),
        load(node_rhs.at[0, 0], node_r),
        load(inverse.at[top], both.at[pl.ds(0, block)]),
    )
    next_in = (
        load(columns, pattern),
        load(rhs.at[pl.ds(n, n)], rhs_v.at[pl.ds(n, n)]),
        load(inverse.at[pl.ds(n, n)], inv_v.at[pl.ds(n, n)]),
        load(factor.at[pl.ds(0, n)], fac_v),
    )
    last_in = (
        load(rhs.at[top], rhs_v.at[low]),
        load(factor.at[top - n], top_fac),
    )
    for copy in first_in:
        copy.wait()
    for r in range(n):
        solved[r] = mm(inv_v[r], rhs_v[r]).astype(BF16)
    for copy in node_in:
        copy.wait()
    lower_mat[...] = mm(node_i[...], node_f[0]).astype(BF16)
    upper = mm(node_i[...], node_f[1]).astype(BF16)
    const[...] = mm(node_i[...], node_r[...])
    both[pl.ds(block, block)] = mm(upper, both[pl.ds(0, block)]).astype(BF16)
    for copy in next_in:
        copy.wait()
    for r in range(n):
        left[r] = leaf_residual(fac_v.at[r], solved, pattern, r, rhs_v[n + r])
    for r in range(n):
        solved[n + r] = mm(inv_v[n + r], left[r]).astype(BF16)
    for copy in last_in:
        copy.wait()
    residual = leaf_residual(top_fac, solved, pattern, top - n, rhs_v[low])
    product = mm(both[...], residual)
    edge[...] = product[:block].astype(BF16)
    down[...] = (const[...] - product[block:]).astype(BF16)


def edge_call(pattern, link, rhs, inverse, factor, node_rhs, node_inverse, node_factor):
    n = LEVEL_ROWS
    coupled, block = factor.shape[1], factor.shape[2]
    loads = rhs.shape[-1]
    return pl.pallas_call(
        edge_kernel,
        out_shape=(
            pltpu.VMEM((2 * n, block, loads), BF16),
            pltpu.VMEM((block, loads), BF16),
            pltpu.VMEM((block, loads), BF16),
            pltpu.VMEM((block, block), BF16),
        ),
        in_specs=[HBM, SMEM] + [HBM] * 6,
        out_specs=(VMEM,) * 4,
        scratch_shapes=[
            pltpu.SMEM(pattern.shape, jnp.int32),
            pltpu.VMEM((2 * n + 1, block, loads), BF16),
            pltpu.VMEM((2 * n, block, block), BF16),
            pltpu.VMEM((n, coupled, block, block), BF16),
            pltpu.VMEM((coupled, block, block), BF16),
            pltpu.VMEM((n, block, loads), BF16),
            pltpu.VMEM((2 * block, block), BF16),
            pltpu.VMEM((block, loads), F32),
            pltpu.VMEM((block, loads), BF16),
            pltpu.VMEM((block, block), BF16),
            pltpu.VMEM((2, block, block), BF16),
            pltpu.SemaphoreType.DMA((12,)),
        ],
        compiler_params=pltpu.CompilerParams(vmem_limit_bytes=16 << 20),
        name="leaf_edge",
    )(
        in_hbm(pattern), link, in_hbm(rhs), in_hbm(inverse), in_hbm(factor),
        in_hbm(node_rhs), in_hbm(node_inverse), in_hbm(node_factor),
    )


def node_zero_kernel(down, lower_mat, lower, *rest):
    rest[-1][...] = (down[...].astype(F32) - mm(lower_mat[...], lower[...])).astype(BF16)


def below_kernel(below, lower_mat, const, out):
    odd = lax.rem(lax.axis_index("rows"), 2) == 1

    @pl.when(odd)
    def _():
        out[...] = const[0]

    @pl.when(jnp.logical_not(odd))
    def _():
        out[...] = const[0] - mm(lower_mat[0], below[...])


def level_one_kernel(part, above, above_mat, edge, inner, lower_mat, upper_mat, out):
    odd = lax.rem(lax.axis_index("rows"), 2) == 1

    @pl.when(odd)
    def _():
        total = part[...] - mm(lower_mat[0], inner[...])
        upper = (above[...].astype(F32) - mm(above_mat[...], edge[...])).astype(BF16)
        out[...] = (total - mm(upper_mat[0], upper)).astype(BF16)

    @pl.when(jnp.logical_not(odd))
    def _():
        out[...] = (part[...] - mm(upper_mat[0], inner[...])).astype(BF16)


def small_call(kernel, name, shape, *args, dtype=BF16):
    return pl.pallas_call(
        kernel,
        out_shape=pltpu.VMEM(shape, dtype),
        in_specs=[VMEM] * len(args),
        out_specs=VMEM,
        compiler_params=pltpu.CompilerParams(vmem_limit_bytes=8 << 20),
        name=name,
    )(*args)


def rest_kernel(columns, rhs, inverse, factor, low, _, top, pattern, rhs_v, inv_v, fac_v, left, sem):
    n = LEVEL_ROWS

    def load(src, dst, slot):
        copy = pltpu.make_async_copy(src, dst, sem.at[slot])
        copy.start()
        return copy

    pattern_in = load(columns, pattern, 0)
    rhs_in = load(rhs.at[pl.ds(2 * n, n)], rhs_v, 1)
    fac_in = [load(factor.at[n + r], fac_v.at[r], 3 + r) for r in range(n)]
    inv_in = load(inverse.at[pl.ds(2 * n, n)], inv_v, 2)
    pattern_in.wait()
    rhs_in.wait()
    for r in range(n):
        fac_in[r].wait()
        left[r] = leaf_residual(fac_v.at[r], low, pattern, n + r, rhs_v[r])
    inv_in.wait()
    for r in range(n):
        top[r] = mm(inv_v[r], left[r]).astype(BF16)


def rest_call(pattern, rhs, inverse, factor, low, after):
    n = LEVEL_ROWS
    coupled, block = factor.shape[1], factor.shape[2]
    loads = rhs.shape[-1]
    flops = 2 * n * (coupled + 1) * block * block * loads
    return pl.pallas_call(
        rest_kernel,
        out_shape=pltpu.VMEM((n, block, loads), BF16),
        in_specs=[HBM] * 4 + [VMEM] * 2,
        out_specs=VMEM,
        scratch_shapes=[
            pltpu.SMEM(pattern.shape, jnp.int32),
            pltpu.VMEM((n, block, loads), BF16),
            pltpu.VMEM((n, block, block), BF16),
            pltpu.VMEM((n, coupled, block, block), BF16),
            pltpu.VMEM((n, block, loads), BF16),
            pltpu.SemaphoreType.DMA((3 + n,)),
        ],
        compiler_params=pltpu.CompilerParams(vmem_limit_bytes=12 << 20),
        cost_estimate=pl.CostEstimate(
            flops=flops, bytes_accessed=36 * block * block * 2, transcendentals=0
        ),
        name="leaf_rest",
    )(in_hbm(pattern), in_hbm(rhs), in_hbm(inverse), in_hbm(factor), low, after)


def fold_kernel(rhs, inverse, factor, _, lower_mat, upper_mat, const):
    for h in range(1, rhs.shape[0]):
        inv = inverse[h, 0]
        lower_mat[h - 1] = mm(inv, factor[h, 0, 0]).astype(BF16)
        upper_mat[h - 1] = mm(inv, factor[h, 0, 1]).astype(BF16)
        const[h - 1] = mm(inv, rhs[h, 0])


def fold_call(rhs, inverse, factor, after):
    depth, _, block, loads = rhs.shape
    depth = depth - 1
    return pl.pallas_call(
        fold_kernel,
        out_shape=(
            pltpu.VMEM((depth, block, block), BF16),
            pltpu.VMEM((depth, block, block), BF16),
            pltpu.VMEM((depth, block, loads), F32),
        ),
        in_specs=[VMEM] * 4,
        out_specs=(VMEM, VMEM, VMEM),
        cost_estimate=pl.CostEstimate(
            flops=6 * depth * block * block * loads,
            bytes_accessed=8 * depth * block * block * 2,
            transcendentals=0,
        ),
        compiler_params=pltpu.CompilerParams(vmem_limit_bytes=16 << 20),
        name="fold",
    )(rhs, inverse, factor, after)


def node_total(h, rows, first, second, lower_mat, upper_mat, const, out, stride, swapped):
    def total(first_mat, second_mat):
        value = const[h, rows] - mm(first_mat[h, rows], first[...])
        out[rows] = (value - mm(second_mat[h, rows], second[...])).astype(BF16)

    if swapped is None:
        total(upper_mat, lower_mat)
        return
    if not swapped:
        total(lower_mat, upper_mat)
        return
    bit = stride_bit(stride)
    pl.when(bit == 1)(lambda: total(lower_mat, upper_mat))
    pl.when(bit == 0)(lambda: total(upper_mat, lower_mat))


def node_kernel(
    h, stride, swapped, first, second, lower_mat, upper_mat, const, *rest
):
    rows = pl.ds(0, const.shape[1])
    node_total(
        h, rows, first, second, lower_mat, upper_mat, const, rest[-1], stride, swapped
    )


def collect_kernel(low, top, *refs):
    *levels, solved, out, sem = refs
    copies = [
        pltpu.make_async_copy(level, out.at[h, 0], sem.at[h]) for h, level in enumerate(levels)
    ]
    n = low.shape[0]
    h = len(levels)
    copies.append(pltpu.make_async_copy(low, solved.at[pl.ds(0, n)], sem.at[h]))
    copies.append(pltpu.make_async_copy(top, solved.at[pl.ds(n, top.shape[0])], sem.at[h + 1]))
    for copy in copies:
        copy.start()
    for copy in copies:
        copy.wait()


def collect_call(low, top, levels, shape):
    rows = low.shape[0] + top.shape[0]
    return pl.pallas_call(
        collect_kernel,
        out_shape=(
            jax.ShapeDtypeStruct((rows,) + low.shape[1:], BF16),
            jax.ShapeDtypeStruct(shape, BF16),
        ),
        in_specs=[VMEM] * (2 + len(levels)),
        out_specs=(HBM, HBM),
        scratch_shapes=[pltpu.SemaphoreType.DMA((2 + len(levels),))],
        compiler_params=pltpu.CompilerParams(vmem_limit_bytes=4 << 20),
        cost_estimate=pl.CostEstimate(
            flops=0,
            bytes_accessed=(rows + len(levels)) * shape[2] * shape[3] * 4,
            transcendentals=0,
        ),
        name="collect",
    )(low, top, *levels)


def last_kernel(
    stride, swapped, first, second, lower_mat, upper_mat, const, _, out, piece, sem
):
    h = const.shape[0] - 1
    size = const.shape[1] // 2
    copies = []
    for half in range(2):
        rows = pl.ds(half * size, size)
        node_total(
            h, rows, first, second, lower_mat, upper_mat, const, piece, stride, swapped
        )
        copy = pltpu.make_async_copy(
            piece.at[rows], out.at[out.shape[0] - 1, 0, rows], sem.at[half]
        )
        copy.start()
        copies.append(copy)
    for copy in copies:
        copy.wait()


def last_call(stride, swapped, first, second, lower_mat, upper_mat, const, collected):
    return pl.pallas_call(
        functools.partial(last_kernel, stride, swapped),
        out_shape=jax.ShapeDtypeStruct(collected.shape, BF16),
        in_specs=[VMEM] * 5 + [HBM],
        out_specs=HBM,
        input_output_aliases={5: 0},
        scratch_shapes=[pltpu.VMEM(first.shape, BF16), pltpu.SemaphoreType.DMA((2,))],
        compiler_params=pltpu.CompilerParams(vmem_limit_bytes=8 << 20),
        name="node_last",
    )(first, second, lower_mat, upper_mat, const, collected)


def shards(
    leaf_rhs,
    separator_rhs,
    leaf_inverse,
    leaf_factor,
    separator_inverse,
    separator_factor,
    block_pattern,
    link_row,
):
    columns = block_pattern.T
    low, edge, down, lower_zero = edge_call(
        columns, link_row, leaf_rhs, leaf_inverse, leaf_factor,
        separator_rhs, separator_inverse, separator_factor,
    )
    shape = edge.shape
    edge_below = passed_along(edge, "rows", 1)
    edge_inner = pair_swap(edge, "rows")
    early = small_call(node_zero_kernel, "level0_early", shape, down, lower_zero, edge_inner)
    below = passed_along(early, "rows", 1)
    above = passed_along(down, "rows", -1)
    above_mat = passed_along(lower_zero, "rows", -1)
    mats = fold_call(separator_rhs, separator_inverse, separator_factor, early)
    block = small_call(
        node_zero_kernel, "level0_late", shape, down, lower_zero, edge_below
    )
    inner = pair_swap(block, "rows")
    levels = [block]
    part = small_call(
        below_kernel, "level1_below", shape, below, mats[0], mats[2], dtype=F32
    )
    block = small_call(
        level_one_kernel, "level1", shape,
        part, above, above_mat, edge, inner, mats[0], mats[1],
    )
    top = rest_call(columns, leaf_rhs, leaf_inverse, leaf_factor, low, block)
    levels.append(block)
    depth = separator_rhs.shape[0]
    for height in range(2, depth):
        stride = 2 ** (height - 1)
        last = height == depth - 1
        swapped = not last
        if swapped:
            first = edge_swap(block, "rows", stride, False)
            second = edge_swap(block, "rows", stride, True)
        else:
            first = passed_along(block, "rows", -stride)
            second = passed_along(block, "rows", stride)
        if not swapped:
            swapped = None
        if not last:
            step = functools.partial(node_kernel, height - 1, stride, swapped)
            block = small_call(step, f"level{height}", shape, first, second, *mats, top)
            levels.append(block)
    solved, collected = collect_call(low, top, levels, (depth, 1) + shape)
    return solved, last_call(stride, swapped, first, second, *mats, collected)


def solution(mesh):
    placed = (
        P("rows", None, None),
        P(None, "rows", None, None),
        P(("draws", "rows"), None, None),
        P(("draws", "rows"), None, None, None),
        P(None, ("draws", "rows"), None, None),
        P(None, ("draws", "rows"), None, None, None),
        P("rows", None),
        P("rows"),
    )
    return jax.shard_map(
        shards,
        mesh=mesh,
        in_specs=placed,
        out_specs=(P(("draws", "rows"), None, None), P(None, ("draws", "rows"), None, None)),
        check_vma=False,
    )
```

```python
import functools

import jax
import jax.numpy as jnp
from jax import lax
from jax.experimental import pallas as pl
from jax.experimental.pallas import tpu as pltpu
from jax.sharding import PartitionSpec as P

LEVEL_ROWS = 4
LEAF_LEVELS = 3
F32 = jnp.float32
BF16 = jnp.bfloat16

SMEM = pl.BlockSpec(memory_space=pltpu.SMEM)
VMEM = pl.BlockSpec(memory_space=pltpu.VMEM)
HBM = pl.BlockSpec(memory_space=pltpu.HBM)


def passed_along(value, axis, by):
    length = lax.axis_size(axis)
    return lax.ppermute(value, axis, [(i, (i + by) % length) for i in range(length)])


def in_hbm(array):
    return pltpu.with_memory_space_constraint(array, pltpu.HBM)


def edge_swap(value, axis, stride, odd):
    length = lax.axis_size(axis)
    pairs = []
    for i in range(length):
        step = stride if (i // stride % 2 == 0) != odd else -stride
        pairs.append((i, (i + step) % length))
    return lax.ppermute(value, axis, pairs)


def stride_bit(stride):
    return lax.rem(lax.div(lax.axis_index("rows"), stride), 2)


def mm(a, b):
    return jnp.dot(a, b, preferred_element_type=F32)


def leaf_residual(factor, solved, pattern, row, rhs):
    coupled = factor.shape[0]
    wide = jnp.concatenate([factor[k] for k in range(coupled)], axis=1)
    tall = jnp.concatenate([solved[pattern[k, row]] for k in range(coupled)], axis=0)
    return (rhs.astype(F32) - mm(wide, tall)).astype(BF16)


def pair_swap(value, axis):
    length = lax.axis_size(axis)
    return lax.ppermute(value, axis, [(i, i ^ 1) for i in range(length)])


def edge_kernel(
    columns, link, rhs, inverse, factor, node_rhs, node_inverse, node_factor,
    solved, edge, down, lower_mat,
    pattern, rhs_v, inv_v, fac_v, top_fac, left, both, const, node_r, node_i, node_f, sem,
):
    n = LEVEL_ROWS
    low = 2 * n
    block = factor.shape[2]
    slots = iter(range(sem.shape[0]))

    def load(src, dst):
        copy = pltpu.make_async_copy(src, dst, sem.at[next(slots)])
        copy.start()
        return copy

    top = link[0]
    first_in = (
        load(inverse.at[pl.ds(0, n)], inv_v.at[pl.ds(0, n)]),
        load(rhs.at[pl.ds(0, n)], rhs_v.at[pl.ds(0, n)]),
    )
    node_in = (
        load(node_inverse.at[0, 0], node_i),
        load(node_factor.at[0, 0], node_f),
        load(node_rhs.at[0, 0], node_r),
        load(inverse.at[top], both.at[pl.ds(0, block)]),
    )
    next_in = (
        load(columns, pattern),
        load(rhs.at[pl.ds(n, n)], rhs_v.at[pl.ds(n, n)]),
        load(inverse.at[pl.ds(n, n)], inv_v.at[pl.ds(n, n)]),
    )
    fac_in = [
        load(factor.at[pl.ds(r, 2)], fac_v.at[pl.ds(r, 2)]) for r in range(0, n, 2)
    ]
    last_in = (
        load(rhs.at[top], rhs_v.at[low]),
        load(factor.at[top - n], top_fac),
    )
    for copy in first_in:
        copy.wait()
    for r in range(n):
        solved[r] = mm(inv_v[r], rhs_v[r]).astype(BF16)
    for copy in node_in:
        copy.wait()
    lower_mat[...] = mm(node_i[...], node_f[0]).astype(BF16)
    upper = mm(node_i[...], node_f[1]).astype(BF16)
    const[...] = mm(node_i[...], node_r[...])
    both[pl.ds(block, block)] = mm(upper, both[pl.ds(0, block)]).astype(BF16)
    for copy in next_in:
        copy.wait()
    for r in range(n):
        if r % 2 == 0:
            fac_in[r // 2].wait()
        left[r] = leaf_residual(fac_v.at[r], solved, pattern, r, rhs_v[n + r])
    for r in range(n):
        solved[n + r] = mm(inv_v[n + r], left[r]).astype(BF16)
    for copy in last_in:
        copy.wait()
    residual = leaf_residual(top_fac, solved, pattern, top - n, rhs_v[low])
    product = mm(both[...], residual)
    edge[...] = product[:block].astype(BF16)
    down[...] = (const[...] - product[block:]).astype(BF16)


def edge_call(pattern, link, rhs, inverse, factor, node_rhs, node_inverse, node_factor):
    n = LEVEL_ROWS
    coupled, block = factor.shape[1], factor.shape[2]
    loads = rhs.shape[-1]
    return pl.pallas_call(
        edge_kernel,
        out_shape=(
            pltpu.VMEM((2 * n, block, loads), BF16),
            pltpu.VMEM((block, loads), BF16),
            pltpu.VMEM((block, loads), BF16),
            pltpu.VMEM((block, block), BF16),
        ),
        in_specs=[HBM, SMEM] + [HBM] * 6,
        out_specs=(VMEM,) * 4,
        scratch_shapes=[
            pltpu.SMEM(pattern.shape, jnp.int32),
            pltpu.VMEM((2 * n + 1, block, loads), BF16),
            pltpu.VMEM((2 * n, block, block), BF16),
            pltpu.VMEM((n, coupled, block, block), BF16),
            pltpu.VMEM((coupled, block, block), BF16),
            pltpu.VMEM((n, block, loads), BF16),
            pltpu.VMEM((2 * block, block), BF16),
            pltpu.VMEM((block, loads), F32),
            pltpu.VMEM((block, loads), BF16),
            pltpu.VMEM((block, block), BF16),
            pltpu.VMEM((2, block, block), BF16),
            pltpu.SemaphoreType.DMA((12 + n,)),
        ],
        compiler_params=pltpu.CompilerParams(vmem_limit_bytes=16 << 20),
        name="leaf_edge",
    )(
        in_hbm(pattern), link, in_hbm(rhs), in_hbm(inverse), in_hbm(factor),
        in_hbm(node_rhs), in_hbm(node_inverse), in_hbm(node_factor),
    )


def node_zero_kernel(down, lower_mat, lower, *rest):
    rest[-1][...] = (down[...].astype(F32) - mm(lower_mat[...], lower[...])).astype(BF16)


def below_kernel(below, lower_mat, const, out):
    odd = lax.rem(lax.axis_index("rows"), 2) == 1

    @pl.when(odd)
    def _():
        out[...] = const[0]

    @pl.when(jnp.logical_not(odd))
    def _():
        out[...] = const[0] - mm(lower_mat[0], below[...])


def level_one_kernel(part, above, above_mat, edge, inner, lower_mat, upper_mat, out):
    odd = lax.rem(lax.axis_index("rows"), 2) == 1

    @pl.when(odd)
    def _():
        total = part[...] - mm(lower_mat[0], inner[...])
        upper = (above[...].astype(F32) - mm(above_mat[...], edge[...])).astype(BF16)
        out[...] = (total - mm(upper_mat[0], upper)).astype(BF16)

    @pl.when(jnp.logical_not(odd))
    def _():
        out[...] = (part[...] - mm(upper_mat[0], inner[...])).astype(BF16)


def small_call(kernel, name, shape, *args, dtype=BF16):
    return pl.pallas_call(
        kernel,
        out_shape=pltpu.VMEM(shape, dtype),
        in_specs=[VMEM] * len(args),
        out_specs=VMEM,
        compiler_params=pltpu.CompilerParams(vmem_limit_bytes=8 << 20),
        name=name,
    )(*args)


def rest_kernel(columns, rhs, inverse, factor, low, _, top, pattern, rhs_v, inv_v, fac_v, left, sem):
    n = LEVEL_ROWS

    def load(src, dst, slot):
        copy = pltpu.make_async_copy(src, dst, sem.at[slot])
        copy.start()
        return copy

    pattern_in = load(columns, pattern, 0)
    rhs_in = load(rhs.at[pl.ds(2 * n, n)], rhs_v, 1)
    fac_in = [load(factor.at[n + r], fac_v.at[r], 3 + r) for r in range(n)]
    inv_in = load(inverse.at[pl.ds(2 * n, n)], inv_v, 2)
    pattern_in.wait()
    rhs_in.wait()
    for r in range(n):
        fac_in[r].wait()
        left[r] = leaf_residual(fac_v.at[r], low, pattern, n + r, rhs_v[r])
    inv_in.wait()
    for r in range(n):
        top[r] = mm(inv_v[r], left[r]).astype(BF16)


def rest_call(pattern, rhs, inverse, factor, low, after):
    n = LEVEL_ROWS
    coupled, block = factor.shape[1], factor.shape[2]
    loads = rhs.shape[-1]
    flops = 2 * n * (coupled + 1) * block * block * loads
    return pl.pallas_call(
        rest_kernel,
        out_shape=pltpu.VMEM((n, block, loads), BF16),
        in_specs=[HBM] * 4 + [VMEM] * 2,
        out_specs=VMEM,
        scratch_shapes=[
            pltpu.SMEM(pattern.shape, jnp.int32),
            pltpu.VMEM((n, block, loads), BF16),
            pltpu.VMEM((n, block, block), BF16),
            pltpu.VMEM((n, coupled, block, block), BF16),
            pltpu.VMEM((n, block, loads), BF16),
            pltpu.SemaphoreType.DMA((3 + n,)),
        ],
        compiler_params=pltpu.CompilerParams(vmem_limit_bytes=12 << 20),
        cost_estimate=pl.CostEstimate(
            flops=flops, bytes_accessed=36 * block * block * 2, transcendentals=0
        ),
        name="leaf_rest",
    )(in_hbm(pattern), in_hbm(rhs), in_hbm(inverse), in_hbm(factor), low, after)


def fold_kernel(rhs, inverse, factor, _, lower_mat, upper_mat, const):
    for h in range(1, rhs.shape[0]):
        inv = inverse[h, 0]
        lower_mat[h - 1] = mm(inv, factor[h, 0, 0]).astype(BF16)
        upper_mat[h - 1] = mm(inv, factor[h, 0, 1]).astype(BF16)
        const[h - 1] = mm(inv, rhs[h, 0])


def fold_call(rhs, inverse, factor, after):
    depth, _, block, loads = rhs.shape
    depth = depth - 1
    return pl.pallas_call(
        fold_kernel,
        out_shape=(
            pltpu.VMEM((depth, block, block), BF16),
            pltpu.VMEM((depth, block, block), BF16),
            pltpu.VMEM((depth, block, loads), F32),
        ),
        in_specs=[VMEM] * 4,
        out_specs=(VMEM, VMEM, VMEM),
        cost_estimate=pl.CostEstimate(
            flops=6 * depth * block * block * loads,
            bytes_accessed=8 * depth * block * block * 2,
            transcendentals=0,
        ),
        compiler_params=pltpu.CompilerParams(vmem_limit_bytes=16 << 20),
        name="fold",
    )(rhs, inverse, factor, after)


def node_total(h, rows, first, second, lower_mat, upper_mat, const, out, stride, swapped):
    def total(first_mat, second_mat):
        value = const[h, rows] - mm(first_mat[h, rows], first[...])
        out[rows] = (value - mm(second_mat[h, rows], second[...])).astype(BF16)

    if swapped is None:
        total(upper_mat, lower_mat)
        return
    if not swapped:
        total(lower_mat, upper_mat)
        return
    bit = stride_bit(stride)
    pl.when(bit == 1)(lambda: total(lower_mat, upper_mat))
    pl.when(bit == 0)(lambda: total(upper_mat, lower_mat))


def node_kernel(
    h, stride, swapped, first, second, lower_mat, upper_mat, const, *rest
):
    rows = pl.ds(0, const.shape[1])
    node_total(
        h, rows, first, second, lower_mat, upper_mat, const, rest[-1], stride, swapped
    )


def collect_kernel(low, top, *refs):
    *levels, solved, out, sem = refs
    copies = [
        pltpu.make_async_copy(level, out.at[h, 0], sem.at[h]) for h, level in enumerate(levels)
    ]
    n = low.shape[0]
    h = len(levels)
    copies.append(pltpu.make_async_copy(low, solved.at[pl.ds(0, n)], sem.at[h]))
    copies.append(pltpu.make_async_copy(top, solved.at[pl.ds(n, top.shape[0])], sem.at[h + 1]))
    for copy in copies:
        copy.start()
    for copy in copies:
        copy.wait()


def collect_call(low, top, levels, shape):
    rows = low.shape[0] + top.shape[0]
    return pl.pallas_call(
        collect_kernel,
        out_shape=(
            jax.ShapeDtypeStruct((rows,) + low.shape[1:], BF16),
            jax.ShapeDtypeStruct(shape, BF16),
        ),
        in_specs=[VMEM] * (2 + len(levels)),
        out_specs=(HBM, HBM),
        scratch_shapes=[pltpu.SemaphoreType.DMA((2 + len(levels),))],
        compiler_params=pltpu.CompilerParams(vmem_limit_bytes=4 << 20),
        cost_estimate=pl.CostEstimate(
            flops=0,
            bytes_accessed=(rows + len(levels)) * shape[2] * shape[3] * 4,
            transcendentals=0,
        ),
        name="collect",
    )(low, top, *levels)


def last_kernel(
    stride, swapped, first, second, lower_mat, upper_mat, const, _, out, piece, sem
):
    h = const.shape[0] - 1
    size = const.shape[1] // 2
    copies = []
    for half in range(2):
        rows = pl.ds(half * size, size)
        node_total(
            h, rows, first, second, lower_mat, upper_mat, const, piece, stride, swapped
        )
        copy = pltpu.make_async_copy(
            piece.at[rows], out.at[out.shape[0] - 1, 0, rows], sem.at[half]
        )
        copy.start()
        copies.append(copy)
    for copy in copies:
        copy.wait()


def last_call(stride, swapped, first, second, lower_mat, upper_mat, const, collected):
    return pl.pallas_call(
        functools.partial(last_kernel, stride, swapped),
        out_shape=jax.ShapeDtypeStruct(collected.shape, BF16),
        in_specs=[VMEM] * 5 + [HBM],
        out_specs=HBM,
        input_output_aliases={5: 0},
        scratch_shapes=[pltpu.VMEM(first.shape, BF16), pltpu.SemaphoreType.DMA((2,))],
        compiler_params=pltpu.CompilerParams(vmem_limit_bytes=8 << 20),
        name="node_last",
    )(first, second, lower_mat, upper_mat, const, collected)


def shards(
    leaf_rhs,
    separator_rhs,
    leaf_inverse,
    leaf_factor,
    separator_inverse,
    separator_factor,
    block_pattern,
    link_row,
):
    columns = block_pattern.T
    low, edge, down, lower_zero = edge_call(
        columns, link_row, leaf_rhs, leaf_inverse, leaf_factor,
        separator_rhs, separator_inverse, separator_factor,
    )
    shape = edge.shape
    edge_below = passed_along(edge, "rows", 1)
    edge_inner = pair_swap(edge, "rows")
    early = small_call(node_zero_kernel, "level0_early", shape, down, lower_zero, edge_inner)
    below = passed_along(early, "rows", 1)
    above = passed_along(down, "rows", -1)
    above_mat = passed_along(lower_zero, "rows", -1)
    mats = fold_call(separator_rhs, separator_inverse, separator_factor, early)
    block = small_call(
        node_zero_kernel, "level0_late", shape, down, lower_zero, edge_below
    )
    inner = pair_swap(block, "rows")
    levels = [block]
    part = small_call(
        below_kernel, "level1_below", shape, below, mats[0], mats[2], dtype=F32
    )
    block = small_call(
        level_one_kernel, "level1", shape,
        part, above, above_mat, edge, inner, mats[0], mats[1],
    )
    top = rest_call(columns, leaf_rhs, leaf_inverse, leaf_factor, low, block)
    levels.append(block)
    depth = separator_rhs.shape[0]
    for height in range(2, depth):
        stride = 2 ** (height - 1)
        last = height == depth - 1
        swapped = not last
        if swapped:
            first = edge_swap(block, "rows", stride, False)
            second = edge_swap(block, "rows", stride, True)
        else:
            first = passed_along(block, "rows", -stride)
            second = passed_along(block, "rows", stride)
        if not swapped:
            swapped = None
        if not last:
            step = functools.partial(node_kernel, height - 1, stride, swapped)
            block = small_call(step, f"level{height}", shape, first, second, *mats, top)
            levels.append(block)
    solved, collected = collect_call(low, top, levels, (depth, 1) + shape)
    return solved, last_call(stride, swapped, first, second, *mats, collected)


def solution(mesh):
    placed = (
        P("rows", None, None),
        P(None, "rows", None, None),
        P(("draws", "rows"), None, None),
        P(("draws", "rows"), None, None, None),
        P(None, ("draws", "rows"), None, None),
        P(None, ("draws", "rows"), None, None, None),
        P("rows", None),
        P("rows"),
    )
    return jax.shard_map(
        shards,
        mesh=mesh,
        in_specs=placed,
        out_specs=(P(("draws", "rows"), None, None), P(None, ("draws", "rows"), None, None)),
        check_vma=False,
    )
```

```python
import functools

import jax
import jax.numpy as jnp
from jax import lax
from jax.experimental import pallas as pl
from jax.experimental.pallas import tpu as pltpu
from jax.sharding import PartitionSpec as P

LEVEL_ROWS = 4
LEAF_LEVELS = 3
F32 = jnp.float32
BF16 = jnp.bfloat16

SMEM = pl.BlockSpec(memory_space=pltpu.SMEM)
VMEM = pl.BlockSpec(memory_space=pltpu.VMEM)
HBM = pl.BlockSpec(memory_space=pltpu.HBM)


def passed_along(value, axis, by):
    length = lax.axis_size(axis)
    return lax.ppermute(value, axis, [(i, (i + by) % length) for i in range(length)])


def in_hbm(array):
    return pltpu.with_memory_space_constraint(array, pltpu.HBM)


def edge_swap(value, axis, stride, odd):
    length = lax.axis_size(axis)
    pairs = []
    for i in range(length):
        step = stride if (i // stride % 2 == 0) != odd else -stride
        pairs.append((i, (i + step) % length))
    return lax.ppermute(value, axis, pairs)


def stride_bit(stride):
    return lax.rem(lax.div(lax.axis_index("rows"), stride), 2)


def mm(a, b):
    return jnp.dot(a, b, preferred_element_type=F32)


def leaf_residual(factor, solved, pattern, row, rhs):
    coupled = factor.shape[0]
    wide = jnp.concatenate([factor[k] for k in range(coupled)], axis=1)
    tall = jnp.concatenate([solved[pattern[k, row]] for k in range(coupled)], axis=0)
    return (rhs.astype(F32) - mm(wide, tall)).astype(BF16)


def pair_swap(value, axis):
    length = lax.axis_size(axis)
    return lax.ppermute(value, axis, [(i, i ^ 1) for i in range(length)])


def edge_kernel(
    columns, link, rhs, inverse, factor, node_rhs, node_inverse, node_factor,
    solved, edge, down, lower_mat,
    pattern, rhs_v, inv_v, fac_v, top_fac, left, both, const, node_r, node_i, node_f, sem,
):
    n = LEVEL_ROWS
    low = 2 * n
    block = factor.shape[2]
    slots = iter(range(sem.shape[0]))

    def load(src, dst):
        copy = pltpu.make_async_copy(src, dst, sem.at[next(slots)])
        copy.start()
        return copy

    top = link[0]
    first_in = (
        load(inverse.at[pl.ds(0, n)], inv_v.at[pl.ds(0, n)]),
        load(rhs.at[pl.ds(0, n)], rhs_v.at[pl.ds(0, n)]),
    )
    node_in = (
        load(node_inverse.at[0, 0], node_i),
        load(node_factor.at[0, 0], node_f),
        load(node_rhs.at[0, 0], node_r),
        load(inverse.at[top], both.at[pl.ds(0, block)]),
    )
    next_in = (
        load(columns, pattern),
        load(rhs.at[pl.ds(n, n)], rhs_v.at[pl.ds(n, n)]),
    )
    fac_in = [
        load(factor.at[pl.ds(r, 2)], fac_v.at[pl.ds(r, 2)]) for r in range(0, n, 2)
    ]
    inv_in = load(inverse.at[pl.ds(n, n)], inv_v.at[pl.ds(n, n)])
    last_in = (
        load(rhs.at[top], rhs_v.at[low]),
        load(factor.at[top - n], top_fac),
    )
    for copy in first_in:
        copy.wait()
    for r in range(n):
        solved[r] = mm(inv_v[r], rhs_v[r]).astype(BF16)
    for copy in node_in:
        copy.wait()
    lower_mat[...] = mm(node_i[...], node_f[0]).astype(BF16)
    upper = mm(node_i[...], node_f[1]).astype(BF16)
    const[...] = mm(node_i[...], node_r[...])
    both[pl.ds(block, block)] = mm(upper, both[pl.ds(0, block)]).astype(BF16)
    for copy in next_in:
        copy.wait()
    for r in range(n):
        if r % 2 == 0:
            fac_in[r // 2].wait()
        left[r] = leaf_residual(fac_v.at[r], solved, pattern, r, rhs_v[n + r])
    inv_in.wait()
    for r in range(n):
        solved[n + r] = mm(inv_v[n + r], left[r]).astype(BF16)
    for copy in last_in:
        copy.wait()
    residual = leaf_residual(top_fac, solved, pattern, top - n, rhs_v[low])
    product = mm(both[...], residual)
    edge[...] = product[:block].astype(BF16)
    down[...] = (const[...] - product[block:]).astype(BF16)


def edge_call(pattern, link, rhs, inverse, factor, node_rhs, node_inverse, node_factor):
    n = LEVEL_ROWS
    coupled, block = factor.shape[1], factor.shape[2]
    loads = rhs.shape[-1]
    return pl.pallas_call(
        edge_kernel,
        out_shape=(
            pltpu.VMEM((2 * n, block, loads), BF16),
            pltpu.VMEM((block, loads), BF16),
            pltpu.VMEM((block, loads), BF16),
            pltpu.VMEM((block, block), BF16),
        ),
        in_specs=[HBM, SMEM] + [HBM] * 6,
        out_specs=(VMEM,) * 4,
        scratch_shapes=[
            pltpu.SMEM(pattern.shape, jnp.int32),
            pltpu.VMEM((2 * n + 1, block, loads), BF16),
            pltpu.VMEM((2 * n, block, block), BF16),
            pltpu.VMEM((n, coupled, block, block), BF16),
            pltpu.VMEM((coupled, block, block), BF16),
            pltpu.VMEM((n, block, loads), BF16),
            pltpu.VMEM((2 * block, block), BF16),
            pltpu.VMEM((block, loads), F32),
            pltpu.VMEM((block, loads), BF16),
            pltpu.VMEM((block, block), BF16),
            pltpu.VMEM((2, block, block), BF16),
            pltpu.SemaphoreType.DMA((12 + n,)),
        ],
        compiler_params=pltpu.CompilerParams(vmem_limit_bytes=16 << 20),
        name="leaf_edge",
    )(
        in_hbm(pattern), link, in_hbm(rhs), in_hbm(inverse), in_hbm(factor),
        in_hbm(node_rhs), in_hbm(node_inverse), in_hbm(node_factor),
    )


def node_zero_kernel(down, lower_mat, lower, *rest):
    rest[-1][...] = (down[...].astype(F32) - mm(lower_mat[...], lower[...])).astype(BF16)


def below_kernel(below, lower_mat, const, out):
    odd = lax.rem(lax.axis_index("rows"), 2) == 1

    @pl.when(odd)
    def _():
        out[...] = const[0]

    @pl.when(jnp.logical_not(odd))
    def _():
        out[...] = const[0] - mm(lower_mat[0], below[...])


def level_one_kernel(part, above, above_mat, edge, inner, lower_mat, upper_mat, out):
    odd = lax.rem(lax.axis_index("rows"), 2) == 1

    @pl.when(odd)
    def _():
        total = part[...] - mm(lower_mat[0], inner[...])
        upper = (above[...].astype(F32) - mm(above_mat[...], edge[...])).astype(BF16)
        out[...] = (total - mm(upper_mat[0], upper)).astype(BF16)

    @pl.when(jnp.logical_not(odd))
    def _():
        out[...] = (part[...] - mm(upper_mat[0], inner[...])).astype(BF16)


def small_call(kernel, name, shape, *args, dtype=BF16):
    return pl.pallas_call(
        kernel,
        out_shape=pltpu.VMEM(shape, dtype),
        in_specs=[VMEM] * len(args),
        out_specs=VMEM,
        compiler_params=pltpu.CompilerParams(vmem_limit_bytes=8 << 20),
        name=name,
    )(*args)


def rest_kernel(columns, rhs, inverse, factor, low, _, top, pattern, rhs_v, inv_v, fac_v, left, sem):
    n = LEVEL_ROWS

    def load(src, dst, slot):
        copy = pltpu.make_async_copy(src, dst, sem.at[slot])
        copy.start()
        return copy

    pattern_in = load(columns, pattern, 0)
    rhs_in = load(rhs.at[pl.ds(2 * n, n)], rhs_v, 1)
    fac_in = [load(factor.at[n + r], fac_v.at[r], 3 + r) for r in range(n)]
    inv_in = load(inverse.at[pl.ds(2 * n, n)], inv_v, 2)
    pattern_in.wait()
    rhs_in.wait()
    for r in range(n):
        fac_in[r].wait()
        left[r] = leaf_residual(fac_v.at[r], low, pattern, n + r, rhs_v[r])
    inv_in.wait()
    for r in range(n):
        top[r] = mm(inv_v[r], left[r]).astype(BF16)


def rest_call(pattern, rhs, inverse, factor, low, after):
    n = LEVEL_ROWS
    coupled, block = factor.shape[1], factor.shape[2]
    loads = rhs.shape[-1]
    flops = 2 * n * (coupled + 1) * block * block * loads
    return pl.pallas_call(
        rest_kernel,
        out_shape=pltpu.VMEM((n, block, loads), BF16),
        in_specs=[HBM] * 4 + [VMEM] * 2,
        out_specs=VMEM,
        scratch_shapes=[
            pltpu.SMEM(pattern.shape, jnp.int32),
            pltpu.VMEM((n, block, loads), BF16),
            pltpu.VMEM((n, block, block), BF16),
            pltpu.VMEM((n, coupled, block, block), BF16),
            pltpu.VMEM((n, block, loads), BF16),
            pltpu.SemaphoreType.DMA((3 + n,)),
        ],
        compiler_params=pltpu.CompilerParams(vmem_limit_bytes=12 << 20),
        cost_estimate=pl.CostEstimate(
            flops=flops, bytes_accessed=36 * block * block * 2, transcendentals=0
        ),
        name="leaf_rest",
    )(in_hbm(pattern), in_hbm(rhs), in_hbm(inverse), in_hbm(factor), low, after)


def fold_kernel(rhs, inverse, factor, _, lower_mat, upper_mat, const):
    for h in range(1, rhs.shape[0]):
        inv = inverse[h, 0]
        lower_mat[h - 1] = mm(inv, factor[h, 0, 0]).astype(BF16)
        upper_mat[h - 1] = mm(inv, factor[h, 0, 1]).astype(BF16)
        const[h - 1] = mm(inv, rhs[h, 0])


def fold_call(rhs, inverse, factor, after):
    depth, _, block, loads = rhs.shape
    depth = depth - 1
    return pl.pallas_call(
        fold_kernel,
        out_shape=(
            pltpu.VMEM((depth, block, block), BF16),
            pltpu.VMEM((depth, block, block), BF16),
            pltpu.VMEM((depth, block, loads), F32),
        ),
        in_specs=[VMEM] * 4,
        out_specs=(VMEM, VMEM, VMEM),
        cost_estimate=pl.CostEstimate(
            flops=6 * depth * block * block * loads,
            bytes_accessed=8 * depth * block * block * 2,
            transcendentals=0,
        ),
        compiler_params=pltpu.CompilerParams(vmem_limit_bytes=16 << 20),
        name="fold",
    )(rhs, inverse, factor, after)


def node_total(h, rows, first, second, lower_mat, upper_mat, const, out, stride, swapped):
    def total(first_mat, second_mat):
        value = const[h, rows] - mm(first_mat[h, rows], first[...])
        out[rows] = (value - mm(second_mat[h, rows], second[...])).astype(BF16)

    if swapped is None:
        total(upper_mat, lower_mat)
        return
    if not swapped:
        total(lower_mat, upper_mat)
        return
    bit = stride_bit(stride)
    pl.when(bit == 1)(lambda: total(lower_mat, upper_mat))
    pl.when(bit == 0)(lambda: total(upper_mat, lower_mat))


def node_kernel(
    h, stride, swapped, first, second, lower_mat, upper_mat, const, *rest
):
    rows = pl.ds(0, const.shape[1])
    node_total(
        h, rows, first, second, lower_mat, upper_mat, const, rest[-1], stride, swapped
    )


def collect_kernel(low, top, *refs):
    *levels, solved, out, sem = refs
    copies = [
        pltpu.make_async_copy(level, out.at[h, 0], sem.at[h]) for h, level in enumerate(levels)
    ]
    n = low.shape[0]
    h = len(levels)
    copies.append(pltpu.make_async_copy(low, solved.at[pl.ds(0, n)], sem.at[h]))
    copies.append(pltpu.make_async_copy(top, solved.at[pl.ds(n, top.shape[0])], sem.at[h + 1]))
    for copy in copies:
        copy.start()
    for copy in copies:
        copy.wait()


def collect_call(low, top, levels, shape):
    rows = low.shape[0] + top.shape[0]
    return pl.pallas_call(
        collect_kernel,
        out_shape=(
            jax.ShapeDtypeStruct((rows,) + low.shape[1:], BF16),
            jax.ShapeDtypeStruct(shape, BF16),
        ),
        in_specs=[VMEM] * (2 + len(levels)),
        out_specs=(HBM, HBM),
        scratch_shapes=[pltpu.SemaphoreType.DMA((2 + len(levels),))],
        compiler_params=pltpu.CompilerParams(vmem_limit_bytes=4 << 20),
        cost_estimate=pl.CostEstimate(
            flops=0,
            bytes_accessed=(rows + len(levels)) * shape[2] * shape[3] * 4,
            transcendentals=0,
        ),
        name="collect",
    )(low, top, *levels)


def last_kernel(
    stride, swapped, first, second, lower_mat, upper_mat, const, _, out, piece, sem
):
    h = const.shape[0] - 1
    size = const.shape[1] // 2
    copies = []
    for half in range(2):
        rows = pl.ds(half * size, size)
        node_total(
            h, rows, first, second, lower_mat, upper_mat, const, piece, stride, swapped
        )
        copy = pltpu.make_async_copy(
            piece.at[rows], out.at[out.shape[0] - 1, 0, rows], sem.at[half]
        )
        copy.start()
        copies.append(copy)
    for copy in copies:
        copy.wait()


def last_call(stride, swapped, first, second, lower_mat, upper_mat, const, collected):
    return pl.pallas_call(
        functools.partial(last_kernel, stride, swapped),
        out_shape=jax.ShapeDtypeStruct(collected.shape, BF16),
        in_specs=[VMEM] * 5 + [HBM],
        out_specs=HBM,
        input_output_aliases={5: 0},
        scratch_shapes=[pltpu.VMEM(first.shape, BF16), pltpu.SemaphoreType.DMA((2,))],
        compiler_params=pltpu.CompilerParams(vmem_limit_bytes=8 << 20),
        name="node_last",
    )(first, second, lower_mat, upper_mat, const, collected)


def shards(
    leaf_rhs,
    separator_rhs,
    leaf_inverse,
    leaf_factor,
    separator_inverse,
    separator_factor,
    block_pattern,
    link_row,
):
    columns = block_pattern.T
    low, edge, down, lower_zero = edge_call(
        columns, link_row, leaf_rhs, leaf_inverse, leaf_factor,
        separator_rhs, separator_inverse, separator_factor,
    )
    shape = edge.shape
    edge_below = passed_along(edge, "rows", 1)
    edge_inner = pair_swap(edge, "rows")
    early = small_call(node_zero_kernel, "level0_early", shape, down, lower_zero, edge_inner)
    below = passed_along(early, "rows", 1)
    above = passed_along(down, "rows", -1)
    above_mat = passed_along(lower_zero, "rows", -1)
    mats = fold_call(separator_rhs, separator_inverse, separator_factor, early)
    block = small_call(
        node_zero_kernel, "level0_late", shape, down, lower_zero, edge_below
    )
    inner = pair_swap(block, "rows")
    levels = [block]
    part = small_call(
        below_kernel, "level1_below", shape, below, mats[0], mats[2], dtype=F32
    )
    block = small_call(
        level_one_kernel, "level1", shape,
        part, above, above_mat, edge, inner, mats[0], mats[1],
    )
    top = rest_call(columns, leaf_rhs, leaf_inverse, leaf_factor, low, block)
    levels.append(block)
    depth = separator_rhs.shape[0]
    for height in range(2, depth):
        stride = 2 ** (height - 1)
        last = height == depth - 1
        swapped = not last
        if swapped:
            first = edge_swap(block, "rows", stride, False)
            second = edge_swap(block, "rows", stride, True)
        else:
            first = passed_along(block, "rows", -stride)
            second = passed_along(block, "rows", stride)
        if not swapped:
            swapped = None
        if not last:
            step = functools.partial(node_kernel, height - 1, stride, swapped)
            block = small_call(step, f"level{height}", shape, first, second, *mats, top)
            levels.append(block)
    solved, collected = collect_call(low, top, levels, (depth, 1) + shape)
    return solved, last_call(stride, swapped, first, second, *mats, collected)


def solution(mesh):
    placed = (
        P("rows", None, None),
        P(None, "rows", None, None),
        P(("draws", "rows"), None, None),
        P(("draws", "rows"), None, None, None),
        P(None, ("draws", "rows"), None, None),
        P(None, ("draws", "rows"), None, None, None),
        P("rows", None),
        P("rows"),
    )
    return jax.shard_map(
        shards,
        mesh=mesh,
        in_specs=placed,
        out_specs=(P(("draws", "rows"), None, None), P(None, ("draws", "rows"), None, None)),
        check_vma=False,
    )
```

```python
import functools

import jax
import jax.numpy as jnp
from jax import lax
from jax.experimental import pallas as pl
from jax.experimental.pallas import tpu as pltpu
from jax.sharding import PartitionSpec as P

LEVEL_ROWS = 4
LEAF_LEVELS = 3
F32 = jnp.float32
BF16 = jnp.bfloat16

SMEM = pl.BlockSpec(memory_space=pltpu.SMEM)
VMEM = pl.BlockSpec(memory_space=pltpu.VMEM)
HBM = pl.BlockSpec(memory_space=pltpu.HBM)


def passed_along(value, axis, by):
    length = lax.axis_size(axis)
    return lax.ppermute(value, axis, [(i, (i + by) % length) for i in range(length)])


def in_hbm(array):
    return pltpu.with_memory_space_constraint(array, pltpu.HBM)


def edge_swap(value, axis, stride, odd):
    length = lax.axis_size(axis)
    pairs = []
    for i in range(length):
        step = stride if (i // stride % 2 == 0) != odd else -stride
        pairs.append((i, (i + step) % length))
    return lax.ppermute(value, axis, pairs)


def stride_bit(stride):
    return lax.rem(lax.div(lax.axis_index("rows"), stride), 2)


def mm(a, b):
    return jnp.dot(a, b, preferred_element_type=F32)


def leaf_residual(factor, solved, pattern, row, rhs):
    coupled = factor.shape[0]
    wide = jnp.concatenate([factor[k] for k in range(coupled)], axis=1)
    tall = jnp.concatenate([solved[pattern[k, row]] for k in range(coupled)], axis=0)
    return (rhs.astype(F32) - mm(wide, tall)).astype(BF16)


def pair_swap(value, axis):
    length = lax.axis_size(axis)
    return lax.ppermute(value, axis, [(i, i ^ 1) for i in range(length)])


def edge_kernel(
    columns, link, rhs, inverse, factor, node_rhs, node_inverse, node_factor,
    solved, edge, down, lower_mat,
    pattern, rhs_v, inv_v, fac_v, top_fac, left, both, const, node_r, node_i, node_f, sem,
):
    n = LEVEL_ROWS
    low = 2 * n
    block = factor.shape[2]
    slots = iter(range(sem.shape[0]))

    def load(src, dst):
        copy = pltpu.make_async_copy(src, dst, sem.at[next(slots)])
        copy.start()
        return copy

    top = link[0]
    first_in = (
        load(inverse.at[pl.ds(0, n)], inv_v.at[pl.ds(0, n)]),
        load(rhs.at[pl.ds(0, n)], rhs_v.at[pl.ds(0, n)]),
    )
    node_in = (
        load(node_inverse.at[0, 0], node_i),
        load(node_factor.at[0, 0], node_f),
        load(node_rhs.at[0, 0], node_r),
        load(inverse.at[top], both.at[pl.ds(0, block)]),
    )
    next_in = (
        load(columns, pattern),
        load(rhs.at[pl.ds(n, n)], rhs_v.at[pl.ds(n, n)]),
    )
    fac_in = [
        load(factor.at[pl.ds(r, 2)], fac_v.at[pl.ds(r, 2)]) for r in range(0, n, 2)
    ]
    inv_in = load(inverse.at[pl.ds(n, n)], inv_v.at[pl.ds(n, n)])
    last_in = (
        load(rhs.at[top], rhs_v.at[low]),
        load(factor.at[top - n], top_fac),
    )
    for copy in first_in:
        copy.wait()
    for r in range(n):
        solved[r] = mm(inv_v[r], rhs_v[r]).astype(BF16)
    for copy in node_in:
        copy.wait()
    lower_mat[...] = mm(node_i[...], node_f[0]).astype(BF16)
    upper = mm(node_i[...], node_f[1]).astype(BF16)
    const[...] = mm(node_i[...], node_r[...])
    both[pl.ds(block, block)] = mm(upper, both[pl.ds(0, block)]).astype(BF16)
    for copy in next_in:
        copy.wait()
    for r in range(n):
        if r % 2 == 0:
            fac_in[r // 2].wait()
        left[r] = leaf_residual(fac_v.at[r], solved, pattern, r, rhs_v[n + r])
    inv_in.wait()
    for r in range(n):
        solved[n + r] = mm(inv_v[n + r], left[r]).astype(BF16)
    for copy in last_in:
        copy.wait()
    residual = leaf_residual(top_fac, solved, pattern, top - n, rhs_v[low])
    product = mm(both[...], residual)
    edge[...] = product[:block].astype(BF16)
    down[...] = (const[...] - product[block:]).astype(BF16)


def edge_call(pattern, link, rhs, inverse, factor, node_rhs, node_inverse, node_factor):
    n = LEVEL_ROWS
    coupled, block = factor.shape[1], factor.shape[2]
    loads = rhs.shape[-1]
    return pl.pallas_call(
        edge_kernel,
        out_shape=(
            pltpu.VMEM((2 * n, block, loads), BF16),
            pltpu.VMEM((block, loads), BF16),
            pltpu.VMEM((block, loads), BF16),
            pltpu.VMEM((block, block), BF16),
        ),
        in_specs=[HBM, SMEM] + [HBM] * 6,
        out_specs=(VMEM,) * 4,
        scratch_shapes=[
            pltpu.SMEM(pattern.shape, jnp.int32),
            pltpu.VMEM((2 * n + 1, block, loads), BF16),
            pltpu.VMEM((2 * n, block, block), BF16),
            pltpu.VMEM((n, coupled, block, block), BF16),
            pltpu.VMEM((coupled, block, block), BF16),
            pltpu.VMEM((n, block, loads), BF16),
            pltpu.VMEM((2 * block, block), BF16),
            pltpu.VMEM((block, loads), F32),
            pltpu.VMEM((block, loads), BF16),
            pltpu.VMEM((block, block), BF16),
            pltpu.VMEM((2, block, block), BF16),
            pltpu.SemaphoreType.DMA((12 + n,)),
        ],
        compiler_params=pltpu.CompilerParams(vmem_limit_bytes=16 << 20),
        name="leaf_edge",
    )(
        in_hbm(pattern), link, in_hbm(rhs), in_hbm(inverse), in_hbm(factor),
        in_hbm(node_rhs), in_hbm(node_inverse), in_hbm(node_factor),
    )


def node_zero_kernel(down, lower_mat, lower, *rest):
    rest[-1][...] = (down[...].astype(F32) - mm(lower_mat[...], lower[...])).astype(BF16)


def below_kernel(below, lower_mat, const, out):
    odd = lax.rem(lax.axis_index("rows"), 2) == 1

    @pl.when(odd)
    def _():
        out[...] = const[0]

    @pl.when(jnp.logical_not(odd))
    def _():
        out[...] = const[0] - mm(lower_mat[0], below[...])


def level_one_kernel(part, above, above_mat, edge, inner, lower_mat, upper_mat, out):
    odd = lax.rem(lax.axis_index("rows"), 2) == 1

    @pl.when(odd)
    def _():
        total = part[...] - mm(lower_mat[0], inner[...])
        upper = (above[...].astype(F32) - mm(above_mat[...], edge[...])).astype(BF16)
        out[...] = (total - mm(upper_mat[0], upper)).astype(BF16)

    @pl.when(jnp.logical_not(odd))
    def _():
        out[...] = (part[...] - mm(upper_mat[0], inner[...])).astype(BF16)


def small_call(kernel, name, shape, *args, dtype=BF16):
    return pl.pallas_call(
        kernel,
        out_shape=pltpu.VMEM(shape, dtype),
        in_specs=[VMEM] * len(args),
        out_specs=VMEM,
        compiler_params=pltpu.CompilerParams(vmem_limit_bytes=8 << 20),
        name=name,
    )(*args)


def rest_kernel(columns, rhs, inverse, factor, low, _, top, pattern, rhs_v, inv_v, fac_v, left, sem):
    n = LEVEL_ROWS

    def load(src, dst, slot):
        copy = pltpu.make_async_copy(src, dst, sem.at[slot])
        copy.start()
        return copy

    pattern_in = load(columns, pattern, 0)
    rhs_in = load(rhs.at[pl.ds(2 * n, n)], rhs_v, 1)
    fac_in = [load(factor.at[n + r], fac_v.at[r], 3 + r) for r in range(n)]
    inv_in = load(inverse.at[pl.ds(2 * n, n)], inv_v, 2)
    pattern_in.wait()
    rhs_in.wait()
    for r in range(n):
        fac_in[r].wait()
        left[r] = leaf_residual(fac_v.at[r], low, pattern, n + r, rhs_v[r])
    inv_in.wait()
    for r in range(n):
        top[r] = mm(inv_v[r], left[r]).astype(BF16)


def rest_call(pattern, rhs, inverse, factor, low, after):
    n = LEVEL_ROWS
    coupled, block = factor.shape[1], factor.shape[2]
    loads = rhs.shape[-1]
    flops = 2 * n * (coupled + 1) * block * block * loads
    return pl.pallas_call(
        rest_kernel,
        out_shape=pltpu.VMEM((n, block, loads), BF16),
        in_specs=[HBM] * 4 + [VMEM] * 2,
        out_specs=VMEM,
        scratch_shapes=[
            pltpu.SMEM(pattern.shape, jnp.int32),
            pltpu.VMEM((n, block, loads), BF16),
            pltpu.VMEM((n, block, block), BF16),
            pltpu.VMEM((n, coupled, block, block), BF16),
            pltpu.VMEM((n, block, loads), BF16),
            pltpu.SemaphoreType.DMA((3 + n,)),
        ],
        compiler_params=pltpu.CompilerParams(vmem_limit_bytes=12 << 20),
        cost_estimate=pl.CostEstimate(
            flops=flops, bytes_accessed=36 * block * block * 2, transcendentals=0
        ),
        name="leaf_rest",
    )(in_hbm(pattern), in_hbm(rhs), in_hbm(inverse), in_hbm(factor), low, after)


def fold_kernel(rhs, inverse, factor, _, lower_mat, upper_mat, const):
    for h in range(1, rhs.shape[0]):
        inv = inverse[h, 0]
        lower_mat[h - 1] = mm(inv, factor[h, 0, 0]).astype(BF16)
        upper_mat[h - 1] = mm(inv, factor[h, 0, 1]).astype(BF16)
        const[h - 1] = mm(inv, rhs[h, 0])


def fold_call(rhs, inverse, factor, after):
    depth, _, block, loads = rhs.shape
    depth = depth - 1
    return pl.pallas_call(
        fold_kernel,
        out_shape=(
            pltpu.VMEM((depth, block, block), BF16),
            pltpu.VMEM((depth, block, block), BF16),
            pltpu.VMEM((depth, block, loads), F32),
        ),
        in_specs=[VMEM] * 4,
        out_specs=(VMEM, VMEM, VMEM),
        cost_estimate=pl.CostEstimate(
            flops=6 * depth * block * block * loads,
            bytes_accessed=8 * depth * block * block * 2,
            transcendentals=0,
        ),
        compiler_params=pltpu.CompilerParams(vmem_limit_bytes=16 << 20),
        name="fold",
    )(rhs, inverse, factor, after)


def node_total(h, rows, first, second, lower_mat, upper_mat, const, out, stride, swapped):
    def total(first_mat, second_mat):
        value = const[h, rows] - mm(first_mat[h, rows], first[...])
        out[rows] = (value - mm(second_mat[h, rows], second[...])).astype(BF16)

    if swapped is None:
        total(upper_mat, lower_mat)
        return
    if not swapped:
        total(lower_mat, upper_mat)
        return
    bit = stride_bit(stride)
    pl.when(bit == 1)(lambda: total(lower_mat, upper_mat))
    pl.when(bit == 0)(lambda: total(upper_mat, lower_mat))


def node_kernel(
    h, stride, swapped, first, second, lower_mat, upper_mat, const, *rest
):
    rows = pl.ds(0, const.shape[1])
    node_total(
        h, rows, first, second, lower_mat, upper_mat, const, rest[-1], stride, swapped
    )


def collect_kernel(low, top, *refs):
    *levels, solved, out, sem = refs
    copies = [
        pltpu.make_async_copy(level, out.at[h, 0], sem.at[h]) for h, level in enumerate(levels)
    ]
    n = low.shape[0]
    h = len(levels)
    copies.append(pltpu.make_async_copy(low, solved.at[pl.ds(0, n)], sem.at[h]))
    copies.append(pltpu.make_async_copy(top, solved.at[pl.ds(n, top.shape[0])], sem.at[h + 1]))
    for copy in copies:
        copy.start()
    for copy in copies:
        copy.wait()


def collect_call(low, top, levels, shape):
    rows = low.shape[0] + top.shape[0]
    return pl.pallas_call(
        collect_kernel,
        out_shape=(
            jax.ShapeDtypeStruct((rows,) + low.shape[1:], BF16),
            jax.ShapeDtypeStruct(shape, BF16),
        ),
        in_specs=[VMEM] * (2 + len(levels)),
        out_specs=(HBM, HBM),
        scratch_shapes=[pltpu.SemaphoreType.DMA((2 + len(levels),))],
        compiler_params=pltpu.CompilerParams(vmem_limit_bytes=4 << 20),
        cost_estimate=pl.CostEstimate(
            flops=0,
            bytes_accessed=(rows + len(levels)) * shape[2] * shape[3] * 4,
            transcendentals=0,
        ),
        name="collect",
    )(low, top, *levels)


def last_kernel(
    stride, swapped, first, second, lower_mat, upper_mat, const, _, out, piece, sem
):
    h = const.shape[0] - 1
    size = const.shape[1] // 2
    copies = []
    for half, rows in enumerate((pl.ds(0, 3 * size // 2), pl.ds(3 * size // 2, size // 2))):
        node_total(
            h, rows, first, second, lower_mat, upper_mat, const, piece, stride, swapped
        )
        copy = pltpu.make_async_copy(
            piece.at[rows], out.at[out.shape[0] - 1, 0, rows], sem.at[half]
        )
        copy.start()
        copies.append(copy)
    for copy in copies:
        copy.wait()


def last_call(stride, swapped, first, second, lower_mat, upper_mat, const, collected):
    return pl.pallas_call(
        functools.partial(last_kernel, stride, swapped),
        out_shape=jax.ShapeDtypeStruct(collected.shape, BF16),
        in_specs=[VMEM] * 5 + [HBM],
        out_specs=HBM,
        input_output_aliases={5: 0},
        scratch_shapes=[pltpu.VMEM(first.shape, BF16), pltpu.SemaphoreType.DMA((2,))],
        compiler_params=pltpu.CompilerParams(vmem_limit_bytes=8 << 20),
        name="node_last",
    )(first, second, lower_mat, upper_mat, const, collected)


def shards(
    leaf_rhs,
    separator_rhs,
    leaf_inverse,
    leaf_factor,
    separator_inverse,
    separator_factor,
    block_pattern,
    link_row,
):
    columns = block_pattern.T
    low, edge, down, lower_zero = edge_call(
        columns, link_row, leaf_rhs, leaf_inverse, leaf_factor,
        separator_rhs, separator_inverse, separator_factor,
    )
    shape = edge.shape
    edge_below = passed_along(edge, "rows", 1)
    edge_inner = pair_swap(edge, "rows")
    early = small_call(node_zero_kernel, "level0_early", shape, down, lower_zero, edge_inner)
    below = passed_along(early, "rows", 1)
    above = passed_along(down, "rows", -1)
    above_mat = passed_along(lower_zero, "rows", -1)
    mats = fold_call(separator_rhs, separator_inverse, separator_factor, early)
    block = small_call(
        node_zero_kernel, "level0_late", shape, down, lower_zero, edge_below
    )
    inner = pair_swap(block, "rows")
    levels = [block]
    part = small_call(
        below_kernel, "level1_below", shape, below, mats[0], mats[2], dtype=F32
    )
    block = small_call(
        level_one_kernel, "level1", shape,
        part, above, above_mat, edge, inner, mats[0], mats[1],
    )
    top = rest_call(columns, leaf_rhs, leaf_inverse, leaf_factor, low, block)
    levels.append(block)
    depth = separator_rhs.shape[0]
    for height in range(2, depth):
        stride = 2 ** (height - 1)
        last = height == depth - 1
        swapped = not last
        if swapped:
            first = edge_swap(block, "rows", stride, False)
            second = edge_swap(block, "rows", stride, True)
        else:
            first = passed_along(block, "rows", -stride)
            second = passed_along(block, "rows", stride)
        if not swapped:
            swapped = None
        if not last:
            step = functools.partial(node_kernel, height - 1, stride, swapped)
            block = small_call(step, f"level{height}", shape, first, second, *mats, top)
            levels.append(block)
    solved, collected = collect_call(low, top, levels, (depth, 1) + shape)
    return solved, last_call(stride, swapped, first, second, *mats, collected)


def solution(mesh):
    placed = (
        P("rows", None, None),
        P(None, "rows", None, None),
        P(("draws", "rows"), None, None),
        P(("draws", "rows"), None, None, None),
        P(None, ("draws", "rows"), None, None),
        P(None, ("draws", "rows"), None, None, None),
        P("rows", None),
        P("rows"),
    )
    return jax.shard_map(
        shards,
        mesh=mesh,
        in_specs=placed,
        out_specs=(P(("draws", "rows"), None, None), P(None, ("draws", "rows"), None, None)),
        check_vma=False,
    )
```
